32 devices in a mesh: dev: 32 (over z, y, x, core).
Axes of the slice: x: 2, y: 2, z: 4, core: 2. Of those that a mesh axis runs over, the one named last changes fastest.
Arguments:
- states: bfloat16 [4096, 1024], P('dev'), may hold values from -400 to 400
- bucket_sizes: int32 [32], P('dev'), may hold values from 1 to 96, 1792 in all
Outputs:
- log_density: float32 [4096], P('dev')
- neighbour_mean: bfloat16 [4096, 1024], P('dev')
The draws below stay inside these ranges and needn't reach their ends.
Inputs may be any that keep to these rules, and one draw needn't show every extreme that they name: `bucket_sizes`: every block holds at least one and at most 96 live states, and some block holds exactly 96.
All inputs are finite; a program needn't handle non-finite values.
Results may differ from the reference program's by a relative error of at most 0.009.
Values may be sent and summed in bfloat16 or wider, within the bound.
No kernel may reach another device: no remote copies, remote signals or barrier semaphores. Data moves between devices by JAX's collectives and lax.ppermute only.
A program may use at most 64 MiB of HBM per device.

```python
import math
import jax
import jax.numpy as jnp
import numpy as np
from jax import lax

D = 1024
BLOCK = 128
LIVE_MAX = 96
NBLOCKS = 32
TOTAL_ROWS = 4096
LIVE_TOTAL = 1792


def draw_states(key, part):
    keys_all = jax.random.split(key, 9)
    col_scale = jnp.exp(jax.random.uniform(keys_all[0], (D,), jnp.float32, 0.0, math.log(10.0)))
    offset_vec = jnp.clip(jax.random.normal(keys_all[1], (D,), jnp.float32), -4.0, 4.0)
    row_place = jnp.arange(TOTAL_ROWS, dtype=jnp.float32) / TOTAL_ROWS
    row_scale = (1.0 + 2.0 * row_place) * jnp.exp(jax.random.uniform(keys_all[2], (TOTAL_ROWS,), jnp.float32, -0.4, 0.4))
    family_count = max(TOTAL_ROWS // 3, 1)
    family_of = jax.random.randint(keys_all[6], (TOTAL_ROWS,), 0, family_count)
    family_vecs = jnp.clip(jax.random.normal(keys_all[7], (family_count, D), jnp.float32), -4.0, 4.0)
    family_share = jax.random.uniform(keys_all[8], (family_count,), jnp.float32, 0.05, 0.8)
    shared = family_vecs[family_of]
    share = family_share[family_of]
    noise_part = jnp.clip(jax.random.normal(keys_all[3], (TOTAL_ROWS, D), jnp.float32), -4.0, 4.0)
    mixed = jnp.sqrt(share)[:, None] * shared + jnp.sqrt(1.0 - share)[:, None] * noise_part
    values = offset_vec[None, :] + row_scale[:, None] * col_scale[None, :] * mixed
    return values.astype(jnp.bfloat16)


def split_up(count, total, most, skew):
    weights = [(1 << 20) // math.isqrt(grade ** skew) + 1 for grade in range(2, count + 1)]
    rest, holding = total - most - (count - 1), [1] * (count - 1)
    while rest > 0:
        movable = [i for i in range(count - 1) if holding[i] < most]
        mass, budget = sum([weights[i] for i in movable]), rest
        for i in movable:
            more = min(most - holding[i], max(1, budget * weights[i] // mass), rest)
            holding[i] = holding[i] + more
            rest = rest - more
    return np.array([most] + holding)


def ragged(stream_key, amount, total, limit, lean):
    if amount == 2:
        one = jax.random.randint(stream_key, (), max(1, total - limit), min(limit, total - 1) + 1)
        return jnp.stack([one, total - one])
    sizes = jnp.asarray(split_up(amount, total, limit, lean), jnp.int32)
    pairs = (amount - 1) // 2
    source_of, receiver = sizes[1:1 + 2 * pairs:2], sizes[2:2 + 2 * pairs:2]
    room = jnp.minimum(source_of - 1, limit - receiver)
    passed = jax.random.randint(jax.random.fold_in(stream_key, 1), (pairs,), 0, 1 << 20) % (room + 1)
    sizes = sizes.at[1:1 + 2 * pairs:2].set(source_of - passed).at[2:2 + 2 * pairs:2].set(receiver + passed)
    return sizes[jax.random.permutation(jax.random.fold_in(stream_key, 2), amount)]


def setup_inputs(seed: int = 0) -> dict:
    key_of = jax.random.split(jax.random.key(seed), 3)
    states = draw_states(jax.random.fold_in(key_of[2], 71), 0)
    bucket_sizes = ragged(key_of[1], NBLOCKS, LIVE_TOTAL, LIVE_MAX, 2).astype(jnp.int32)
    return {"states": states, "bucket_sizes": bucket_sizes}


EPS = 1e-06
RIDGE = 1.0

def reference(states, bucket_sizes):
    total_rows, feature_dim = states.shape
    position = jnp.arange(total_rows, dtype=jnp.int32)
    block_of = position // BLOCK
    live_mask = (position % BLOCK < bucket_sizes[block_of]).astype(jnp.float32)
    live_count = jnp.sum(bucket_sizes).astype(jnp.float32)
    widened = states.astype(jnp.float32)
    mean_vec = lax.optimization_barrier(jnp.sum(widened * live_mask[:, None], axis=0)) / live_count
    centred = (widened - mean_vec) * live_mask[:, None]
    covariance = jnp.dot(centred.T, centred, precision=lax.Precision.HIGHEST) / live_count
    covariance = covariance + RIDGE * jnp.eye(feature_dim, dtype=jnp.float32)
    factor = jnp.linalg.cholesky(covariance)
    white = jax.scipy.linalg.solve_triangular(factor, (widened - mean_vec).T, lower=True).T.astype(jnp.bfloat16)
    white_f = white.astype(jnp.float32)
    inverse_norm = lax.rsqrt(lax.optimization_barrier(jnp.sum(white_f * white_f, axis=1)) + EPS)
    sharpness = 2.0 * math.sqrt(feature_dim)
    query_blocks = total_rows // BLOCK

    def one_block(args):
        query_white, query_norm, query_rows = args
        inner_prod = jnp.einsum('qd,kd->qk', query_white.astype(jnp.float32), white.astype(jnp.float32), preferred_element_type=jnp.float32)
        scores = sharpness * (query_norm[:, None] * inverse_norm[None, :] * inner_prod - 1.0)
        other = (query_rows[:, None] != position[None, :]).astype(jnp.float32)
        weights = jnp.exp(scores) * live_mask[None, :] * other
        density = lax.optimization_barrier(jnp.sum(weights, axis=1))
        neighbour_sum = jnp.dot(weights.astype(jnp.bfloat16).astype(jnp.float32), white.astype(jnp.float32), preferred_element_type=jnp.float32)
        return (density, neighbour_sum)
    density, neighbour_sum = lax.map(one_block, (white.reshape(query_blocks, BLOCK, feature_dim), inverse_norm.reshape(query_blocks, BLOCK), position.reshape(query_blocks, BLOCK)))
    density = density.reshape(total_rows)
    neighbour_sum = neighbour_sum.reshape(total_rows, feature_dim)
    is_live = live_mask > 0.5
    log_density = jnp.where(is_live, jnp.log(density), 0.0).astype(jnp.float32)
    neighbour_mean = jnp.where(is_live[:, None], neighbour_sum / density[:, None], 0.0).astype(jnp.bfloat16)
    return (log_density, neighbour_mean)
```

```python
import math

import jax
import jax.numpy as jnp
from jax import lax
from jax.experimental import pallas as pl
from jax.experimental.pallas import tpu as pltpu
from jax.sharding import PartitionSpec as P

EPS = 1e-06
RIDGE = 1.0
LIVE_MAX = 96
DEAD = 1024.0
DEAD_ABOVE = 512.0
SUB = 8
LANES = 128
TILE = 256
CHUNK = 512
VMEM_BYTES = 60 << 20
EXACT = lax.Precision.HIGHEST


def product(left, right, left_dim, right_dim, precision=None):
    return lax.dot_general(
        left,
        right,
        (((left_dim,), (right_dim,)), ((), ())),
        precision=precision,
        preferred_element_type=jnp.float32,
    )


def two_parts(value):
    high = value.astype(jnp.bfloat16)
    return high, (value - high.astype(jnp.float32)).astype(jnp.bfloat16)


def chunk_of(rows):
    return math.gcd(rows, CHUNK)


def moments_kernel(keys_ref, mean_ref, cov_ref, total):
    rows, dim = keys_ref.shape
    step = chunk_of(rows)
    tiles = dim // TILE

    def live_of(block):
        return block[:, :1] < DEAD_ABOVE

    def add_sums(index, carry):
        sums, count = carry
        block = keys_ref[pl.ds(pl.multiple_of(index * step, step), step), :].astype(jnp.float32)
        live = live_of(block)
        part = jnp.where(live, block, 0.0).reshape(step // SUB, SUB, dim)
        alive = live.astype(jnp.float32).reshape(step // SUB, SUB, 1)
        return sums + jnp.sum(part, axis=0), count + jnp.sum(alive, axis=0)

    start = (jnp.zeros((SUB, dim), jnp.float32), jnp.zeros((SUB, 1), jnp.float32))
    sums, count = lax.fori_loop(0, rows // step, add_sums, start)
    count = jnp.sum(count, axis=0, keepdims=True)
    mean = jnp.sum(sums, axis=0, keepdims=True) / count
    mean_ref[...] = jnp.broadcast_to(mean, (SUB, dim))
    total[...] = jnp.zeros_like(total)

    @pl.loop(0, rows // step)
    def _(index):
        block = keys_ref[pl.ds(pl.multiple_of(index * step, step), step), :].astype(jnp.float32)
        high, low = two_parts(jnp.where(live_of(block), block - mean, 0.0))
        for tile in range(tiles):
            here = slice(tile * TILE, (tile + 1) * TILE)
            upto = slice(0, (tile + 1) * TILE)
            part = product(high[:, here], high[:, upto], 0, 0)
            part += product(high[:, here], low[:, upto], 0, 0)
            part += product(low[:, here], high[:, upto], 0, 0)
            total[here, upto] += part

    for tile in range(tiles):
        here = slice(tile * TILE, (tile + 1) * TILE)
        upto = slice(0, (tile + 1) * TILE)
        shape = (TILE, (tile + 1) * TILE)
        down = lax.broadcasted_iota(jnp.int32, shape, 0) + tile * TILE
        across = lax.broadcasted_iota(jnp.int32, shape, 1)
        cov_ref[here, upto] = total[here, upto] / count + jnp.where(down == across, RIDGE, 0.0)


def invert_factor(rows, inverse):
    count = len(rows)
    sublane = lax.broadcasted_iota(jnp.int32, (SUB, LANES), 0)

    def over_lanes(value, lane):
        return jnp.broadcast_to(value[:, lane : lane + 1], (SUB, LANES))

    def over_sublanes(value, row):
        return jnp.broadcast_to(value[row : row + 1, :], (SUB, LANES))

    for step in range(count):
        first = SUB * step
        pivot_rows, inverse_rows = rows[step], inverse[step]
        columns = [over_lanes(pivot_rows, first + t) for t in range(SUB)]
        below = {
            i: [over_lanes(rows[i], first + t) for t in range(SUB)]
            for i in range(step + 1, count)
        }
        scale, entry, upper, solved = [], {}, [], []
        for t in range(SUB):
            root = lax.rsqrt(over_sublanes(columns[t], t))
            scale.append(root)
            down = jnp.where(sublane > t, columns[t] * root, 0.0)
            upper.append(over_sublanes(pivot_rows, t) * root)
            solved.append(over_sublanes(inverse_rows, t) * root)
            for q in range(t + 1, SUB):
                entry[q, t] = over_sublanes(columns[q], t) * root
                columns[q] = columns[q] - down * entry[q, t]
            pivot_rows = pivot_rows - down * upper[t]
            inverse_rows = jnp.where(sublane == t, solved[t], inverse_rows - down * solved[t])
        inverse[step] = inverse_rows
        for i in range(step + 1, count):
            column, row, other = below[i], rows[i], inverse[i]
            for t in range(SUB):
                factor = column[t] * scale[t]
                for q in range(t + 1, SUB):
                    column[q] = column[q] - factor * entry[q, t]
                row = row - factor * upper[t]
                other = other - factor * solved[t]
            rows[i], inverse[i] = row, other
    return inverse


def whitener_kernel(cov_ref, high_ref, low_ref, work, found, block, part):
    dim = cov_ref.shape[0]
    work[...] = cov_ref[...]
    found[...] = jnp.zeros_like(found)
    block[...] = cov_ref[0:LANES, 0:LANES]
    count = LANES // SUB

    @pl.loop(0, dim // LANES)
    def _(index):
        lane = lax.broadcasted_iota(jnp.int32, (SUB, LANES), 1)
        sublane = lax.broadcasted_iota(jnp.int32, (SUB, LANES), 0)
        rows = [block[SUB * i : SUB * i + SUB, :] for i in range(count)]
        inverse = [(lane == sublane + SUB * i).astype(jnp.float32) for i in range(count)]
        inverse = invert_factor(rows, inverse)
        for i in range(count):
            part[SUB * i : SUB * i + SUB, :] = inverse[i]
        for here in range(dim // LANES):
            top = here // 2 * TILE
            mid, end = top + LANES, top + TILE

            @pl.when(index == here)
            def _(here=here, top=top, mid=mid, end=end):
                own = part[...]
                if here % 2 == 0:
                    left = product(work[mid:end, top:mid], own, 1, 1, EXACT)
                    block[...] = work[mid:end, mid:end] - product(left, left, 1, 1, EXACT)
                    found[top:mid, top:mid] = own
                    found[mid:end, top:mid] = product(left, own, 1, 0, EXACT)
                    return
                found[mid:end, mid:end] = own
                found[mid:end, top:mid] = -product(own, found[mid:end, top:mid], 1, 0, EXACT)
                pair = found[top:end, top:end]
                if end < dim:
                    panel = product(work[end:dim, top:end], pair, 1, 1, EXACT)
                    for low in range(0, dim - end, TILE):
                        size = low + TILE
                        strip = slice(end + low, end + size)
                        work[strip, end : end + size] = work[strip, end : end + size] - product(
                            panel[low:size], panel[0:size], 1, 1, EXACT
                        )
                    block[...] = work[end : end + LANES, end : end + LANES]
                if top > 0:
                    found[top:end, 0:top] = product(pair, found[top:end, 0:top], 1, 0, EXACT)
                if end < dim:
                    found[end:dim, 0:end] = found[end:dim, 0:end] - product(
                        panel, found[top:end, 0:end], 1, 0, EXACT
                    )

    high, low = two_parts(found[...])
    high_ref[...] = high
    low_ref[...] = low


def scores_kernel(
    place_ref, keys_ref, own_ref, mean_ref, high_ref, low_ref, log_ref, out_ref, density, total
):
    rows, dim = keys_ref.shape
    queries = own_ref.shape[0]
    step = chunk_of(rows)
    sharpness = 2.0 * math.sqrt(dim)
    mean = mean_ref[0:1, :]

    def whitened(values):
        high, low = two_parts(values.astype(jnp.float32) - mean)
        parts = []
        for tile in range(dim // TILE):
            here = slice(tile * TILE, (tile + 1) * TILE)
            upto = slice(0, (tile + 1) * TILE)
            part = product(high[:, upto], high_ref[here, upto], 1, 1)
            part += product(high[:, upto], low_ref[here, upto], 1, 1)
            part += product(low[:, upto], high_ref[here, upto], 1, 1)
            parts.append(part.astype(jnp.bfloat16))
        return jnp.concatenate(parts, axis=1)

    def lengths(white):
        wide = white.astype(jnp.float32)
        return lax.rsqrt(jnp.sum(wide * wide, axis=1, keepdims=True) + EPS)

    query = whitened(own_ref[...])
    query_norm = jnp.broadcast_to(lengths(query), (queries, queries)).T[0:1, :]
    density[...] = jnp.zeros_like(density)
    total[...] = jnp.zeros_like(total)

    @pl.loop(0, rows // step)
    def _(index):
        start = pl.multiple_of(index * step, step)
        block = keys_ref[pl.ds(start, step), :]
        live = block[:, :1].astype(jnp.float32) < DEAD_ABOVE
        white = whitened(block)
        inner = product(white, query, 1, 1)
        scores = sharpness * (lengths(white) * query_norm * inner - 1.0)
        shape = (step, queries)
        key_index = start + lax.broadcasted_iota(jnp.int32, shape, 0)
        query_index = place_ref[0] + lax.broadcasted_iota(jnp.int32, shape, 1)
        seen = live & (key_index != query_index)
        weights = jnp.where(seen, jnp.exp(scores), 0.0)
        density[...] += jnp.sum(weights, axis=0, keepdims=True)
        total[...] += product(weights.astype(jnp.bfloat16), white, 0, 0)

    own_size = place_ref[1]
    dense = density[...]
    lane = lax.broadcasted_iota(jnp.int32, dense.shape, 1)
    log_ref[...] = jnp.where(lane < own_size, jnp.log(dense), 0.0)
    divisor = jnp.broadcast_to(dense, (queries, queries)).T[:, 0:1]
    sublane = lax.broadcasted_iota(jnp.int32, (queries, 1), 0)
    out_ref[...] = jnp.where(sublane < own_size, total[...] / divisor, 0.0).astype(jnp.bfloat16)


def whole(count):
    return [pl.BlockSpec(memory_space=pltpu.VMEM)] * count


def shards(states, bucket_sizes):
    row_count, dim = states.shape
    block_count = bucket_sizes.shape[0]
    block_rows = row_count // block_count
    params = pltpu.CompilerParams(vmem_limit_bytes=VMEM_BYTES)
    square = (dim, dim)
    in_block = jnp.arange(LIVE_MAX, dtype=jnp.int32)
    own_live = (in_block[None, :] < bucket_sizes[:, None])[:, :, None]
    prefix = states.reshape(block_count, block_rows, dim)[:, :LIVE_MAX]
    sent = jnp.where(own_live, prefix, jnp.bfloat16(DEAD)).reshape(-1, dim)
    keys = lax.all_gather(sent, "dev", axis=0, tiled=True)
    mean, covariance = pl.pallas_call(
        moments_kernel,
        out_shape=[
            jax.ShapeDtypeStruct((SUB, dim), jnp.float32),
            jax.ShapeDtypeStruct(square, jnp.float32),
        ],
        in_specs=whole(1),
        out_specs=whole(2),
        scratch_shapes=[pltpu.VMEM(square, jnp.float32)],
        compiler_params=params,
    )(keys)
    high, low = pl.pallas_call(
        whitener_kernel,
        out_shape=[jax.ShapeDtypeStruct(square, jnp.bfloat16)] * 2,
        in_specs=whole(1),
        out_specs=whole(2),
        scratch_shapes=[
            pltpu.VMEM(square, jnp.float32),
            pltpu.VMEM(square, jnp.float32),
            pltpu.VMEM((LANES, LANES), jnp.float32),
            pltpu.VMEM((LANES, LANES), jnp.float32),
        ],
        compiler_params=params,
    )(covariance)
    logs, means = [], []
    for here in range(block_count):
        place = (lax.axis_index("dev") * block_count + here) * LIVE_MAX
        log_part, mean_part = pl.pallas_call(
            scores_kernel,
            out_shape=[
                jax.ShapeDtypeStruct((1, block_rows), jnp.float32),
                jax.ShapeDtypeStruct((block_rows, dim), jnp.bfloat16),
            ],
            in_specs=[pl.BlockSpec(memory_space=pltpu.SMEM)] + whole(5),
            out_specs=whole(2),
            scratch_shapes=[
                pltpu.VMEM((1, block_rows), jnp.float32),
                pltpu.VMEM((block_rows, dim), jnp.float32),
            ],
            compiler_params=params,
        )(
            jnp.stack([place, bucket_sizes[here]]),
            keys,
            lax.slice_in_dim(states, here * block_rows, (here + 1) * block_rows),
            mean,
            high,
            low,
        )
        logs.append(log_part.reshape(block_rows))
        means.append(mean_part)
    return jnp.concatenate(logs), jnp.concatenate(means)


def solution(mesh):
    placed = (P("dev", None), P("dev"))
    return jax.shard_map(
        shards, mesh=mesh, in_specs=placed, out_specs=(P("dev"), P("dev", None)), check_vma=False
    )
```

```python
import math

import jax
import jax.numpy as jnp
from jax import lax
from jax.experimental import pallas as pl
from jax.experimental.pallas import tpu as pltpu
from jax.sharding import PartitionSpec as P

EPS = 1e-06
RIDGE = 1.0
LIVE_MAX = 96
DEAD = 1024.0
DEAD_ABOVE = 512.0
SUB = 8
LANES = 128
TILE = 256
CHUNK = 512
VMEM_BYTES = 60 << 20
EXACT = lax.Precision.HIGHEST


def product(left, right, left_dim, right_dim, precision=None):
    return lax.dot_general(
        left,
        right,
        (((left_dim,), (right_dim,)), ((), ())),
        precision=precision,
        preferred_element_type=jnp.float32,
    )


def two_parts(value):
    high = value.astype(jnp.bfloat16)
    return high, (value - high.astype(jnp.float32)).astype(jnp.bfloat16)


def flipped(value, mask):
    size = lax.axis_size("dev")
    return lax.ppermute(value, "dev", [(source, source ^ mask) for source in range(size)])


def gather_rows(rows):
    size = lax.axis_size("dev")
    near, far = size // 4, size // 2
    across = flipped(rows, far)
    beside = flipped(rows, near)
    groups = [rows, across, beside, flipped(across, near)]
    pieces = []
    for group in groups:
        pieces.append(group)
        pieces += [flipped(group, mask) for mask in range(2, near, 2)]
    same_core = jnp.concatenate(pieces, axis=0)
    return jnp.concatenate([same_core, flipped(same_core, 1)], axis=0)


def chunk_of(rows):
    return math.gcd(rows, CHUNK)


def moments_kernel(keys_ref, mean_ref, cov_ref, total):
    rows, dim = keys_ref.shape
    step = chunk_of(rows)
    tiles = dim // TILE

    def live_of(block):
        return block[:, :1] < DEAD_ABOVE

    def add_sums(index, carry):
        sums, count = carry
        block = keys_ref[pl.ds(pl.multiple_of(index * step, step), step), :].astype(jnp.float32)
        live = live_of(block)
        part = jnp.where(live, block, 0.0).reshape(step // SUB, SUB, dim)
        alive = live.astype(jnp.float32).reshape(step // SUB, SUB, 1)
        return sums + jnp.sum(part, axis=0), count + jnp.sum(alive, axis=0)

    start = (jnp.zeros((SUB, dim), jnp.float32), jnp.zeros((SUB, 1), jnp.float32))
    sums, count = lax.fori_loop(0, rows // step, add_sums, start)
    count = jnp.sum(count, axis=0, keepdims=True)
    mean = jnp.sum(sums, axis=0, keepdims=True) / count
    mean_ref[...] = jnp.broadcast_to(mean, (SUB, dim))
    total[...] = jnp.zeros_like(total)

    @pl.loop(0, rows // step)
    def _(index):
        block = keys_ref[pl.ds(pl.multiple_of(index * step, step), step), :].astype(jnp.float32)
        high, low = two_parts(jnp.where(live_of(block), block - mean, 0.0))
        for tile in range(tiles):
            here = slice(tile * TILE, (tile + 1) * TILE)
            upto = slice(0, (tile + 1) * TILE)
            part = product(high[:, here], high[:, upto], 0, 0)
            part += product(high[:, here], low[:, upto], 0, 0)
            part += product(low[:, here], high[:, upto], 0, 0)
            total[here, upto] += part

    for tile in range(tiles):
        here = slice(tile * TILE, (tile + 1) * TILE)
        upto = slice(0, (tile + 1) * TILE)
        shape = (TILE, (tile + 1) * TILE)
        down = lax.broadcasted_iota(jnp.int32, shape, 0) + tile * TILE
        across = lax.broadcasted_iota(jnp.int32, shape, 1)
        cov_ref[here, upto] = total[here, upto] / count + jnp.where(down == across, RIDGE, 0.0)


def invert_factor(rows, inverse):
    count = len(rows)
    sublane = lax.broadcasted_iota(jnp.int32, (SUB, LANES), 0)

    def over_lanes(value, lane):
        return jnp.broadcast_to(value[:, lane : lane + 1], (SUB, LANES))

    def over_sublanes(value, row):
        return jnp.broadcast_to(value[row : row + 1, :], (SUB, LANES))

    for step in range(count):
        first = SUB * step
        pivot_rows, inverse_rows = rows[step], inverse[step]
        columns = [over_lanes(pivot_rows, first + t) for t in range(SUB)]
        below = {
            i: [over_lanes(rows[i], first + t) for t in range(SUB)]
            for i in range(step + 1, count)
        }
        scale, entry, upper, solved = [], {}, [], []
        for t in range(SUB):
            root = lax.rsqrt(over_sublanes(columns[t], t))
            scale.append(root)
            down = jnp.where(sublane > t, columns[t] * root, 0.0)
            upper.append(over_sublanes(pivot_rows, t) * root)
            solved.append(over_sublanes(inverse_rows, t) * root)
            for q in range(t + 1, SUB):
                entry[q, t] = over_sublanes(columns[q], t) * root
                columns[q] = columns[q] - down * entry[q, t]
            pivot_rows = pivot_rows - down * upper[t]
            inverse_rows = jnp.where(sublane == t, solved[t], inverse_rows - down * solved[t])
        inverse[step] = inverse_rows
        for i in range(step + 1, count):
            column, row, other = below[i], rows[i], inverse[i]
            for t in range(SUB):
                factor = column[t] * scale[t]
                for q in range(t + 1, SUB):
                    column[q] = column[q] - factor * entry[q, t]
                row = row - factor * upper[t]
                other = other - factor * solved[t]
            rows[i], inverse[i] = row, other
    return inverse


def whitener_kernel(cov_ref, high_ref, low_ref, work, found, block, part):
    dim = cov_ref.shape[0]
    work[...] = cov_ref[...]
    found[...] = jnp.zeros_like(found)
    block[...] = cov_ref[0:LANES, 0:LANES]
    count = LANES // SUB

    @pl.loop(0, dim // LANES)
    def _(index):
        lane = lax.broadcasted_iota(jnp.int32, (SUB, LANES), 1)
        sublane = lax.broadcasted_iota(jnp.int32, (SUB, LANES), 0)
        rows = [block[SUB * i : SUB * i + SUB, :] for i in range(count)]
        inverse = [(lane == sublane + SUB * i).astype(jnp.float32) for i in range(count)]
        inverse = invert_factor(rows, inverse)
        for i in range(count):
            part[SUB * i : SUB * i + SUB, :] = inverse[i]
        for here in range(dim // LANES):
            top = here // 2 * TILE
            mid, end = top + LANES, top + TILE

            @pl.when(index == here)
            def _(here=here, top=top, mid=mid, end=end):
                own = part[...]
                if here % 2 == 0:
                    left = product(work[mid:end, top:mid], own, 1, 1, EXACT)
                    block[...] = work[mid:end, mid:end] - product(left, left, 1, 1, EXACT)
                    found[top:mid, top:mid] = own
                    found[mid:end, top:mid] = product(left, own, 1, 0, EXACT)
                    return
                found[mid:end, mid:end] = own
                found[mid:end, top:mid] = -product(own, found[mid:end, top:mid], 1, 0, EXACT)
                pair = found[top:end, top:end]
                if end < dim:
                    panel = product(work[end:dim, top:end], pair, 1, 1, EXACT)
                    for low in range(0, dim - end, TILE):
                        size = low + TILE
                        strip = slice(end + low, end + size)
                        work[strip, end : end + size] = work[strip, end : end + size] - product(
                            panel[low:size], panel[0:size], 1, 1, EXACT
                        )
                    block[...] = work[end : end + LANES, end : end + LANES]
                if top > 0:
                    found[top:end, 0:top] = product(pair, found[top:end, 0:top], 1, 0, EXACT)
                if end < dim:
                    found[end:dim, 0:end] = found[end:dim, 0:end] - product(
                        panel, found[top:end, 0:end], 1, 0, EXACT
                    )

    high, low = two_parts(found[...])
    high_ref[...] = high
    low_ref[...] = low


def scores_kernel(
    place_ref, keys_ref, own_ref, mean_ref, high_ref, low_ref, log_ref, out_ref, density, total
):
    rows, dim = keys_ref.shape
    queries = own_ref.shape[0]
    step = chunk_of(rows)
    sharpness = 2.0 * math.sqrt(dim)
    mean = mean_ref[0:1, :]

    def whitened(values):
        high, low = two_parts(values.astype(jnp.float32) - mean)
        parts = []
        for tile in range(dim // TILE):
            here = slice(tile * TILE, (tile + 1) * TILE)
            upto = slice(0, (tile + 1) * TILE)
            part = product(high[:, upto], high_ref[here, upto], 1, 1)
            part += product(high[:, upto], low_ref[here, upto], 1, 1)
            part += product(low[:, upto], high_ref[here, upto], 1, 1)
            parts.append(part.astype(jnp.bfloat16))
        return jnp.concatenate(parts, axis=1)

    def lengths(white):
        wide = white.astype(jnp.float32)
        return lax.rsqrt(jnp.sum(wide * wide, axis=1, keepdims=True) + EPS)

    query = whitened(own_ref[...])
    query_norm = jnp.broadcast_to(lengths(query), (queries, queries)).T[0:1, :]
    density[...] = jnp.zeros_like(density)
    total[...] = jnp.zeros_like(total)

    @pl.loop(0, rows // step)
    def _(index):
        start = pl.multiple_of(index * step, step)
        block = keys_ref[pl.ds(start, step), :]
        live = block[:, :1].astype(jnp.float32) < DEAD_ABOVE
        white = whitened(block)
        inner = product(white, query, 1, 1)
        scores = sharpness * (lengths(white) * query_norm * inner - 1.0)
        shape = (step, queries)
        key_index = start + lax.broadcasted_iota(jnp.int32, shape, 0)
        query_index = place_ref[0] + lax.broadcasted_iota(jnp.int32, shape, 1)
        seen = live & (key_index != query_index)
        weights = jnp.where(seen, jnp.exp(scores), 0.0)
        density[...] += jnp.sum(weights, axis=0, keepdims=True)
        total[...] += product(weights.astype(jnp.bfloat16), white, 0, 0)

    own_size = place_ref[1]
    dense = density[...]
    lane = lax.broadcasted_iota(jnp.int32, dense.shape, 1)
    log_ref[...] = jnp.where(lane < own_size, jnp.log(dense), 0.0)
    divisor = jnp.broadcast_to(dense, (queries, queries)).T[:, 0:1]
    sublane = lax.broadcasted_iota(jnp.int32, (queries, 1), 0)
    out_ref[...] = jnp.where(sublane < own_size, total[...] / divisor, 0.0).astype(jnp.bfloat16)


def whole(count):
    return [pl.BlockSpec(memory_space=pltpu.VMEM)] * count


def shards(states, bucket_sizes):
    row_count, dim = states.shape
    block_count = bucket_sizes.shape[0]
    block_rows = row_count // block_count
    params = pltpu.CompilerParams(vmem_limit_bytes=VMEM_BYTES)
    square = (dim, dim)
    in_block = jnp.arange(LIVE_MAX, dtype=jnp.int32)
    own_live = (in_block[None, :] < bucket_sizes[:, None])[:, :, None]
    prefix = states.reshape(block_count, block_rows, dim)[:, :LIVE_MAX]
    sent = jnp.where(own_live, prefix, jnp.bfloat16(DEAD)).reshape(-1, dim)
    keys = gather_rows(sent)
    mean, covariance = pl.pallas_call(
        moments_kernel,
        out_shape=[
            jax.ShapeDtypeStruct((SUB, dim), jnp.float32),
            jax.ShapeDtypeStruct(square, jnp.float32),
        ],
        in_specs=whole(1),
        out_specs=whole(2),
        scratch_shapes=[pltpu.VMEM(square, jnp.float32)],
        compiler_params=params,
    )(keys)
    high, low = pl.pallas_call(
        whitener_kernel,
        out_shape=[jax.ShapeDtypeStruct(square, jnp.bfloat16)] * 2,
        in_specs=whole(1),
        out_specs=whole(2),
        scratch_shapes=[
            pltpu.VMEM(square, jnp.float32),
            pltpu.VMEM(square, jnp.float32),
            pltpu.VMEM((LANES, LANES), jnp.float32),
            pltpu.VMEM((LANES, LANES), jnp.float32),
        ],
        compiler_params=params,
    )(covariance)
    logs, means = [], []
    for here in range(block_count):
        place = jnp.int32(here * LIVE_MAX)
        log_part, mean_part = pl.pallas_call(
            scores_kernel,
            out_shape=[
                jax.ShapeDtypeStruct((1, block_rows), jnp.float32),
                jax.ShapeDtypeStruct((block_rows, dim), jnp.bfloat16),
            ],
            in_specs=[pl.BlockSpec(memory_space=pltpu.SMEM)] + whole(5),
            out_specs=whole(2),
            scratch_shapes=[
                pltpu.VMEM((1, block_rows), jnp.float32),
                pltpu.VMEM((block_rows, dim), jnp.float32),
            ],
            compiler_params=params,
        )(
            jnp.stack([place, bucket_sizes[here]]),
            keys,
            lax.slice_in_dim(states, here * block_rows, (here + 1) * block_rows),
            mean,
            high,
            low,
        )
        logs.append(log_part.reshape(block_rows))
        means.append(mean_part)
    return jnp.concatenate(logs), jnp.concatenate(means)


def solution(mesh):
    placed = (P("dev", None), P("dev"))
    return jax.shard_map(
        shards, mesh=mesh, in_specs=placed, out_specs=(P("dev"), P("dev", None)), check_vma=False
    )
```

```python
import functools
import math

import jax
import jax.numpy as jnp
from jax import lax
from jax.experimental import pallas as pl
from jax.experimental.pallas import tpu as pltpu
from jax.sharding import PartitionSpec as P

EPS = 1e-06
RIDGE = 1.0
LIVE_MAX = 96
DEAD = 1024.0
DEAD_ABOVE = 512.0
SUB = 8
LANES = 128
TILE = 256
PACK = 16
CHUNK = 512
REST = 128
VMEM_BYTES = 60 << 20
EXACT = lax.Precision.HIGHEST


def product(left, right, left_dim, right_dim, precision=None):
    return lax.dot_general(
        left,
        right,
        (((left_dim,), (right_dim,)), ((), ())),
        precision=precision,
        preferred_element_type=jnp.float32,
    )


def two_parts(value):
    high = value.astype(jnp.bfloat16)
    return high, (value - high.astype(jnp.float32)).astype(jnp.bfloat16)


def flipped(value, mask):
    size = lax.axis_size("dev")
    return lax.ppermute(value, "dev", [(source, source ^ mask) for source in range(size)])


def plane_of(group, near, direct):
    if near != 8 or direct:
        return [group] + [flipped(group, mask) for mask in range(2, near, 2)]
    half = group.shape[0] // 2
    side, ahead = flipped(group, 2), flipped(group, 4)
    return [group, side, ahead, flipped(side[:half], 4), flipped(ahead[half:], 2)]


def gather_rows(rows):
    size = lax.axis_size("dev")
    near, far = size // 4, size // 2
    across, beside = flipped(rows, far), flipped(rows, near)
    groups = [rows, across, beside, flipped(across, near)]
    same_core = [
        jnp.concatenate(plane_of(group, near, place == 3), axis=0)
        for place, group in enumerate(groups)
    ]
    return same_core + [flipped(group, 1) for group in same_core]


def live_of(block):
    return block[:, :1].astype(jnp.float32) < DEAD_ABOVE


def over_chunks(rows, body):
    whole = rows // CHUNK

    @pl.loop(0, whole)
    def _(index):
        body(pl.multiple_of(index * CHUNK, CHUNK), CHUNK)

    @pl.loop(whole * (CHUNK // REST), pl.cdiv(rows, REST))
    def _(index):
        body(pl.multiple_of(index * REST, REST), REST)


def collect(groups, keys, counts, sizes, starts, arrived, copied):
    blocks = keys.shape[0] // LIVE_MAX
    copies, first = [], 0
    for place, group in enumerate(groups):
        rows = group.shape[0]
        copies.append(
            pltpu.make_async_copy(group, keys.at[pl.ds(first, rows)], arrived.at[place])
        )
        copies[-1].start()
        first += rows
    first = 0
    for place, group in enumerate(groups):
        copies[place].wait()
        last = first + group.shape[0] // LIVE_MAX

        @pl.loop(first, last)
        def _(block):
            start = pl.multiple_of(block * LIVE_MAX, PACK)
            marks = keys[pl.ds(start, LIVE_MAX), :LANES].astype(jnp.float32)
            alive = jnp.sum((marks < DEAD_ABOVE).astype(jnp.float32), axis=0, keepdims=True)
            counts[pl.ds(block, 1), :] = alive.astype(jnp.int32)

        first = last
    copy = pltpu.make_async_copy(counts, sizes, copied)
    copy.start()
    copy.wait()

    def move_block(block, carry):
        offset, count = carry
        size = sizes[block, 0]
        tiles = (size + PACK - 1) // PACK
        starts[block] = offset

        def move_tile(tile, unused):
            source = pl.multiple_of(block * LIVE_MAX + tile * PACK, PACK)
            target = pl.multiple_of(offset + tile * PACK, PACK)
            keys[pl.ds(target, PACK), :] = keys[pl.ds(source, PACK), :]
            return unused

        lax.fori_loop(0, tiles, move_tile, 0)
        return offset + tiles * PACK, count + size

    rows, count = lax.fori_loop(0, blocks, move_block, (jnp.int32(0), jnp.int32(0)))

    @pl.loop(rows // PACK, pl.cdiv(rows, REST) * (REST // PACK))
    def _(tile):
        target = pl.multiple_of(tile * PACK, PACK)
        keys[pl.ds(target, PACK), :] = jnp.full((PACK, keys.shape[1]), DEAD, keys.dtype)

    return rows, count


def moments(keys, rows, count, mean_ref, work):
    dim = keys.shape[1]
    tiles = dim // TILE

    def add_sums(index, sums):
        start = pl.multiple_of(index * REST, REST)
        block = keys[pl.ds(start, REST), :]
        part = jnp.where(live_of(block), block.astype(jnp.float32), 0.0)
        return sums + jnp.sum(part.reshape(REST // SUB, SUB, dim), axis=0)

    sums = lax.fori_loop(0, pl.cdiv(rows, REST), add_sums, jnp.zeros((SUB, dim), jnp.float32))
    count = jnp.full((1, 1), count.astype(jnp.float32))
    mean = jnp.sum(sums, axis=0, keepdims=True) / count
    mean_ref[...] = mean
    work[...] = jnp.zeros_like(work)

    def add_products(start, step):
        block = keys[pl.ds(start, step), :]
        centred = jnp.where(live_of(block), block.astype(jnp.float32) - mean_ref[...], 0.0)
        high, low = two_parts(centred)
        for tile in range(tiles):
            here = slice(tile * TILE, (tile + 1) * TILE)
            upto = slice(0, (tile + 1) * TILE)
            part = product(high[:, here], high[:, upto], 0, 0)
            part += product(high[:, here], low[:, upto], 0, 0)
            part += product(low[:, here], high[:, upto], 0, 0)
            work[here, upto] += part

    over_chunks(rows, add_products)
    for tile in range(tiles):
        here = slice(tile * TILE, (tile + 1) * TILE)
        upto = slice(0, (tile + 1) * TILE)
        shape = (TILE, (tile + 1) * TILE)
        down = lax.broadcasted_iota(jnp.int32, shape, 0) + tile * TILE
        across = lax.broadcasted_iota(jnp.int32, shape, 1)
        work[here, upto] = work[here, upto] / count + jnp.where(down == across, RIDGE, 0.0)


def invert_factor(rows, inverse):
    count = len(rows)
    sublane = lax.broadcasted_iota(jnp.int32, (SUB, LANES), 0)

    def over_lanes(value, lane):
        return jnp.broadcast_to(value[:, lane : lane + 1], (SUB, LANES))

    def over_sublanes(value, row):
        return jnp.broadcast_to(value[row : row + 1, :], (SUB, LANES))

    for step in range(count):
        first = SUB * step
        pivot_rows, inverse_rows = rows[step], inverse[step]
        columns = [over_lanes(pivot_rows, first + t) for t in range(SUB)]
        below = {
            i: [over_lanes(rows[i], first + t) for t in range(SUB)]
            for i in range(step + 1, count)
        }
        scale, entry, upper, solved = [], {}, [], []
        for t in range(SUB):
            root = lax.rsqrt(over_sublanes(columns[t], t))
            scale.append(root)
            down = jnp.where(sublane > t, columns[t] * root, 0.0)
            upper.append(over_sublanes(pivot_rows, t) * root)
            solved.append(over_sublanes(inverse_rows, t) * root)
            for q in range(t + 1, SUB):
                entry[q, t] = over_sublanes(columns[q], t) * root
                columns[q] = columns[q] - down * entry[q, t]
            pivot_rows = pivot_rows - down * upper[t]
            inverse_rows = jnp.where(sublane == t, solved[t], inverse_rows - down * solved[t])
        inverse[step] = inverse_rows
        for i in range(step + 1, count):
            column, row, other = below[i], rows[i], inverse[i]
            for t in range(SUB):
                factor = column[t] * scale[t]
                for q in range(t + 1, SUB):
                    column[q] = column[q] - factor * entry[q, t]
                row = row - factor * upper[t]
                other = other - factor * solved[t]
            rows[i], inverse[i] = row, other
    return inverse


def whitener(work, found, block, part, high_ref, low_ref):
    dim = work.shape[0]
    found[...] = jnp.zeros_like(found)
    block[...] = work[0:LANES, 0:LANES]
    count = LANES // SUB

    @pl.loop(0, dim // LANES)
    def _(index):
        lane = lax.broadcasted_iota(jnp.int32, (SUB, LANES), 1)
        sublane = lax.broadcasted_iota(jnp.int32, (SUB, LANES), 0)
        rows = [block[SUB * i : SUB * i + SUB, :] for i in range(count)]
        inverse = [(lane == sublane + SUB * i).astype(jnp.float32) for i in range(count)]
        inverse = invert_factor(rows, inverse)
        for i in range(count):
            part[SUB * i : SUB * i + SUB, :] = inverse[i]
        for here in range(dim // LANES):
            top = here // 2 * TILE
            mid, end = top + LANES, top + TILE

            @pl.when(index == here)
            def _(here=here, top=top, mid=mid, end=end):
                own = part[...]
                if here % 2 == 0:
                    left = product(work[mid:end, top:mid], own, 1, 1, EXACT)
                    block[...] = work[mid:end, mid:end] - product(left, left, 1, 1, EXACT)
                    found[top:mid, top:mid] = own
                    found[mid:end, top:mid] = product(left, own, 1, 0, EXACT)
                    return
                found[mid:end, mid:end] = own
                found[mid:end, top:mid] = -product(own, found[mid:end, top:mid], 1, 0, EXACT)
                pair = found[top:end, top:end]
                if end < dim:
                    panel = product(work[end:dim, top:end], pair, 1, 1, EXACT)
                    for low in range(0, dim - end, TILE):
                        size = low + TILE
                        strip = slice(end + low, end + size)
                        work[strip, end : end + size] = work[strip, end : end + size] - product(
                            panel[low:size], panel[0:size], 1, 1, EXACT
                        )
                    block[...] = work[end : end + LANES, end : end + LANES]
                if top > 0:
                    found[top:end, 0:top] = product(pair, found[top:end, 0:top], 1, 0, EXACT)
                if end < dim:
                    found[end:dim, 0:end] = found[end:dim, 0:end] - product(
                        panel, found[top:end, 0:end], 1, 0, EXACT
                    )

    high, low = two_parts(found[...])
    high_ref[...] = high
    low_ref[...] = low


def scores(keys, rows, own_ref, own_size, own_start, mean_ref, high_ref, low_ref, density, total):
    dim = keys.shape[1]
    queries = own_ref.shape[0]
    sharpness = 2.0 * math.sqrt(dim)

    def whitened(values):
        high, low = two_parts(values.astype(jnp.float32) - mean_ref[...])
        parts = []
        for tile in range(dim // TILE):
            here = slice(tile * TILE, (tile + 1) * TILE)
            upto = slice(0, (tile + 1) * TILE)
            part = product(high[:, upto], high_ref[here, upto], 1, 1)
            part += product(high[:, upto], low_ref[here, upto], 1, 1)
            part += product(low[:, upto], high_ref[here, upto], 1, 1)
            parts.append(part.astype(jnp.bfloat16))
        return jnp.concatenate(parts, axis=1)

    def lengths(white):
        wide = white.astype(jnp.float32)
        return lax.rsqrt(jnp.sum(wide * wide, axis=1, keepdims=True) + EPS)

    query = whitened(own_ref[...])
    query_norm = jnp.broadcast_to(lengths(query), (queries, queries)).T[0:1, :]
    density[...] = jnp.zeros_like(density)
    total[...] = jnp.zeros_like(total)

    def add_keys(start, step):
        block = keys[pl.ds(start, step), :]
        white = whitened(block)
        inner = product(white, query, 1, 1)
        scores = sharpness * (lengths(white) * query_norm * inner - 1.0)
        shape = (step, queries)
        key_index = start + lax.broadcasted_iota(jnp.int32, shape, 0)
        query_index = own_start + lax.broadcasted_iota(jnp.int32, shape, 1)
        seen = live_of(block) & (key_index != query_index)
        weights = jnp.where(seen, jnp.exp(scores), 0.0)
        density[...] += jnp.sum(weights, axis=0, keepdims=True)
        total[...] += product(weights.astype(jnp.bfloat16), white, 0, 0)

    over_chunks(rows, add_keys)
    dense = density[...]
    lane = lax.broadcasted_iota(jnp.int32, dense.shape, 1)
    logs = jnp.where(lane < own_size, jnp.log(dense), 0.0)
    divisor = jnp.broadcast_to(dense, (queries, queries)).T[:, 0:1]
    sublane = lax.broadcasted_iota(jnp.int32, (queries, 1), 0)
    means = jnp.where(sublane < own_size, total[...] / divisor, 0.0).astype(jnp.bfloat16)
    return logs, means


def local_kernel(group_count, size_ref, own_ref, *refs):
    groups, refs = refs[:group_count], refs[group_count:]
    log_ref, out_ref, keys, counts, sizes, starts, arrived, copied = refs[:8]
    mean_ref, work, found, block, part, high_ref, low_ref, density, total = refs[8:]
    rows, count = collect(groups, keys, counts, sizes, starts, arrived, copied)
    moments(keys, rows, count, mean_ref, work)
    whitener(work, found, block, part, high_ref, low_ref)
    block_count = size_ref.shape[0]
    block_rows = own_ref.shape[0] // block_count
    for here in range(block_count):
        span = slice(here * block_rows, (here + 1) * block_rows)
        log_ref[here : here + 1, :], out_ref[span, :] = scores(
            keys,
            rows,
            own_ref.at[span],
            size_ref[here],
            starts[here],
            mean_ref,
            high_ref,
            low_ref,
            density,
            total,
        )


def shards(states, bucket_sizes):
    row_count, dim = states.shape
    block_count = bucket_sizes.shape[0]
    block_rows = row_count // block_count
    in_block = jnp.arange(LIVE_MAX, dtype=jnp.int32)
    own_live = (in_block[None, :] < bucket_sizes[:, None])[:, :, None]
    prefix = states.reshape(block_count, block_rows, dim)[:, :LIVE_MAX]
    sent = jnp.where(own_live, prefix, jnp.bfloat16(DEAD)).reshape(-1, dim)
    groups = gather_rows(sent)
    key_rows = sum(group.shape[0] for group in groups)
    blocks = key_rows // LIVE_MAX
    square = (dim, dim)
    logs, means = pl.pallas_call(
        functools.partial(local_kernel, len(groups)),
        out_shape=[
            jax.ShapeDtypeStruct((block_count, block_rows), jnp.float32),
            jax.ShapeDtypeStruct((row_count, dim), jnp.bfloat16),
        ],
        in_specs=[
            pl.BlockSpec(memory_space=pltpu.SMEM),
            pl.BlockSpec(memory_space=pltpu.VMEM),
        ]
        + [pl.BlockSpec(memory_space=pl.ANY)] * len(groups),
        out_specs=[pl.BlockSpec(memory_space=pltpu.VMEM)] * 2,
        scratch_shapes=[
            pltpu.VMEM((key_rows, dim), jnp.bfloat16),
            pltpu.VMEM((blocks, LANES), jnp.int32),
            pltpu.SMEM((blocks, LANES), jnp.int32),
            pltpu.SMEM((blocks,), jnp.int32),
            pltpu.SemaphoreType.DMA((len(groups),)),
            pltpu.SemaphoreType.DMA,
            pltpu.VMEM((1, dim), jnp.float32),
            pltpu.VMEM(square, jnp.float32),
            pltpu.VMEM(square, jnp.float32),
            pltpu.VMEM((LANES, LANES), jnp.float32),
            pltpu.VMEM((LANES, LANES), jnp.float32),
            pltpu.VMEM(square, jnp.bfloat16),
            pltpu.VMEM(square, jnp.bfloat16),
            pltpu.VMEM((1, block_rows), jnp.float32),
            pltpu.VMEM((block_rows, dim), jnp.float32),
        ],
        compiler_params=pltpu.CompilerParams(vmem_limit_bytes=VMEM_BYTES),
    )(bucket_sizes, states, *groups)
    return logs.reshape(row_count), means


def solution(mesh):
    placed = (P("dev", None), P("dev"))
    return jax.shard_map(
        shards, mesh=mesh, in_specs=placed, out_specs=(P("dev"), P("dev", None)), check_vma=False
    )
```

```python
import functools
import math

import jax
import jax.numpy as jnp
from jax import lax
from jax.experimental import pallas as pl
from jax.experimental.pallas import tpu as pltpu
from jax.sharding import PartitionSpec as P

EPS = 1e-06
RIDGE = 1.0
LIVE_MAX = 96
DEAD = 1024.0
DEAD_ABOVE = 512.0
SUB = 8
LANES = 128
TILE = 256
PACK = 16
CHUNK = 512
REST = 256
VMEM_BYTES = 60 << 20
EXACT = lax.Precision.HIGHEST


def product(left, right, left_dim, right_dim, precision=None):
    return lax.dot_general(
        left,
        right,
        (((left_dim,), (right_dim,)), ((), ())),
        precision=precision,
        preferred_element_type=jnp.float32,
    )


def two_parts(value):
    high = value.astype(jnp.bfloat16)
    return high, (value - high.astype(jnp.float32)).astype(jnp.bfloat16)


def three_products(left, right):
    left_high, left_low = two_parts(left)
    right_high, right_low = two_parts(right)
    return (
        product(left_high, right_high, 1, 0)
        + product(left_high, right_low, 1, 0)
        + product(left_low, right_high, 1, 0)
    )


def flipped(value, mask):
    size = lax.axis_size("dev")
    return lax.ppermute(value, "dev", [(source, source ^ mask) for source in range(size)])


def plane_of(group, near, direct):
    if near != 8 or direct:
        return [group] + [flipped(group, mask) for mask in range(2, near, 2)]
    half = group.shape[0] // 2
    side, ahead = flipped(group, 2), flipped(group, 4)
    return [group, side, ahead, flipped(side[:half], 4), flipped(ahead[half:], 2)]


def gather_rows(rows):
    size = lax.axis_size("dev")
    near, far = size // 4, size // 2
    across, beside = flipped(rows, far), flipped(rows, near)
    groups = [rows, across, beside, flipped(across, near)]
    same_core = [
        jnp.concatenate(plane_of(group, near, place == 3), axis=0)
        for place, group in enumerate(groups)
    ]
    return same_core + [flipped(group, 1) for group in same_core]


def live_of(block):
    return block[:, :1].astype(jnp.float32) < DEAD_ABOVE


def over_chunks(rows, body):
    whole = (rows + (CHUNK - REST - 1)) // CHUNK

    @pl.loop(0, whole)
    def _(index):
        body(pl.multiple_of(index * CHUNK, CHUNK), CHUNK)

    @pl.when(whole * CHUNK < rows)
    def _():
        body(pl.multiple_of(whole * CHUNK, CHUNK), REST)


def collect(groups, keys, counts, sizes, starts, arrived, copied):
    blocks = keys.shape[0] // LIVE_MAX
    copies, first = [], 0
    for place, group in enumerate(groups):
        rows = group.shape[0]
        copies.append(
            pltpu.make_async_copy(group, keys.at[pl.ds(first, rows)], arrived.at[place])
        )
        copies[-1].start()
        first += rows
    first = 0
    for place, group in enumerate(groups):
        copies[place].wait()
        last = first + group.shape[0] // LIVE_MAX

        @pl.loop(first, last)
        def _(block):
            start = pl.multiple_of(block * LIVE_MAX, PACK)
            marks = keys[pl.ds(start, LIVE_MAX), :LANES].astype(jnp.float32)
            alive = jnp.sum((marks < DEAD_ABOVE).astype(jnp.float32), axis=0, keepdims=True)
            counts[pl.ds(block, 1), :] = alive.astype(jnp.int32)

        first = last
    copy = pltpu.make_async_copy(counts, sizes, copied)
    copy.start()
    copy.wait()

    def move_block(block, carry):
        offset, count = carry
        size = sizes[block, 0]
        tiles = (size + PACK - 1) // PACK
        starts[block] = offset

        def move_tile(tile, unused):
            source = pl.multiple_of(block * LIVE_MAX + tile * PACK, PACK)
            target = pl.multiple_of(offset + tile * PACK, PACK)
            keys[pl.ds(target, PACK), :] = keys[pl.ds(source, PACK), :]
            return unused

        lax.fori_loop(0, tiles, move_tile, 0)
        return offset + tiles * PACK, count + size

    rows, count = lax.fori_loop(0, blocks, move_block, (jnp.int32(0), jnp.int32(0)))

    @pl.loop(rows // PACK, pl.cdiv(rows, REST) * (REST // PACK))
    def _(tile):
        target = pl.multiple_of(tile * PACK, PACK)
        keys[pl.ds(target, PACK), :] = jnp.full((PACK, keys.shape[1]), DEAD, keys.dtype)

    return rows, count


def moments(keys, rows, count, mean_ref, work):
    dim = keys.shape[1]
    tiles = dim // TILE

    def add_sums(index, sums):
        start = pl.multiple_of(index * REST, REST)
        block = keys[pl.ds(start, REST), :]
        part = jnp.where(live_of(block), block.astype(jnp.float32), 0.0)
        return sums + jnp.sum(part.reshape(REST // SUB, SUB, dim), axis=0)

    sums = lax.fori_loop(0, pl.cdiv(rows, REST), add_sums, jnp.zeros((SUB, dim), jnp.float32))
    count = jnp.full((1, 1), count.astype(jnp.float32))
    mean = jnp.sum(sums, axis=0, keepdims=True) / count
    mean_ref[...] = mean
    work[...] = jnp.zeros_like(work)

    def add_products(start, step):
        block = keys[pl.ds(start, step), :]
        centred = jnp.where(live_of(block), block.astype(jnp.float32) - mean_ref[...], 0.0)
        high, low = two_parts(centred)
        for tile in range(tiles):
            here = slice(tile * TILE, (tile + 1) * TILE)
            upto = slice(0, (tile + 1) * TILE)
            part = product(high[:, here], high[:, upto], 0, 0)
            part += product(high[:, here], low[:, upto], 0, 0)
            part += product(low[:, here], high[:, upto], 0, 0)
            work[here, upto] += part

    over_chunks(rows, add_products)
    for tile in range(tiles):
        here = slice(tile * TILE, (tile + 1) * TILE)
        upto = slice(0, (tile + 1) * TILE)
        shape = (TILE, (tile + 1) * TILE)
        down = lax.broadcasted_iota(jnp.int32, shape, 0) + tile * TILE
        across = lax.broadcasted_iota(jnp.int32, shape, 1)
        work[here, upto] = work[here, upto] / count + jnp.where(down == across, RIDGE, 0.0)


def invert_factor(rows, inverse):
    count = len(rows)
    sublane = lax.broadcasted_iota(jnp.int32, (SUB, LANES), 0)

    def over_lanes(value, lane):
        return jnp.broadcast_to(value[:, lane : lane + 1], (SUB, LANES))

    def over_sublanes(value, row):
        return jnp.broadcast_to(value[row : row + 1, :], (SUB, LANES))

    for step in range(count):
        first = SUB * step
        pivot_rows, inverse_rows = rows[step], inverse[step]
        columns = [over_lanes(pivot_rows, first + t) for t in range(SUB)]
        below = {
            i: [over_lanes(rows[i], first + t) for t in range(SUB)]
            for i in range(step + 1, count)
        }
        scale, entry, upper, solved = [], {}, [], []
        for t in range(SUB):
            root = lax.rsqrt(over_sublanes(columns[t], t))
            scale.append(root)
            down = jnp.where(sublane > t, columns[t] * root, 0.0)
            upper.append(over_sublanes(pivot_rows, t) * root)
            solved.append(over_sublanes(inverse_rows, t) * root)
            for q in range(t + 1, SUB):
                entry[q, t] = over_sublanes(columns[q], t) * root
                columns[q] = columns[q] - down * entry[q, t]
            pivot_rows = pivot_rows - down * upper[t]
            inverse_rows = jnp.where(sublane == t, solved[t], inverse_rows - down * solved[t])
        inverse[step] = inverse_rows
        for i in range(step + 1, count):
            column, row, other = below[i], rows[i], inverse[i]
            for t in range(SUB):
                factor = column[t] * scale[t]
                for q in range(t + 1, SUB):
                    column[q] = column[q] - factor * entry[q, t]
                row = row - factor * upper[t]
                other = other - factor * solved[t]
            rows[i], inverse[i] = row, other
    return inverse


def whitener(work, found, block, part, high_ref, low_ref):
    dim = work.shape[0]
    found[...] = jnp.zeros_like(found)
    block[...] = work[0:LANES, 0:LANES]
    count = LANES // SUB

    @pl.loop(0, dim // LANES)
    def _(index):
        lane = lax.broadcasted_iota(jnp.int32, (SUB, LANES), 1)
        sublane = lax.broadcasted_iota(jnp.int32, (SUB, LANES), 0)
        rows = [block[SUB * i : SUB * i + SUB, :] for i in range(count)]
        inverse = [(lane == sublane + SUB * i).astype(jnp.float32) for i in range(count)]
        inverse = invert_factor(rows, inverse)
        for i in range(count):
            part[SUB * i : SUB * i + SUB, :] = inverse[i]
        for here in range(dim // LANES):
            top = here // 2 * TILE
            mid, end = top + LANES, top + TILE

            @pl.when(index == here)
            def _(here=here, top=top, mid=mid, end=end):
                own = part[...]
                if here % 2 == 0:
                    left = product(work[mid:end, top:mid], own, 1, 1, EXACT)
                    block[...] = work[mid:end, mid:end] - product(left, left, 1, 1, EXACT)
                    found[top:mid, top:mid] = own
                    found[mid:end, top:mid] = product(left, own, 1, 0, EXACT)
                    return
                found[mid:end, mid:end] = own
                found[mid:end, top:mid] = -product(own, found[mid:end, top:mid], 1, 0, EXACT)
                pair = found[top:end, top:end]
                if end < dim:
                    panel = product(work[end:dim, top:end], pair, 1, 1, EXACT)
                    for low in range(0, dim - end, TILE):
                        size = low + TILE
                        strip = slice(end + low, end + size)
                        work[strip, end : end + size] = work[strip, end : end + size] - product(
                            panel[low:size], panel[0:size], 1, 1, EXACT
                        )
                    block[...] = work[end : end + LANES, end : end + LANES]
                if top > 0:
                    found[top:end, 0:top] = three_products(pair, found[top:end, 0:top])
                if end < dim:
                    found[end:dim, 0:end] = found[end:dim, 0:end] - three_products(
                        panel, found[top:end, 0:end]
                    )

    high, low = two_parts(found[...])
    high_ref[...] = high
    low_ref[...] = low


def scores(keys, rows, own_ref, own_size, own_start, mean_ref, high_ref, low_ref, density, total):
    dim = keys.shape[1]
    queries = own_ref.shape[0]
    sharpness = 2.0 * math.sqrt(dim)

    def whitened(values):
        high, low = two_parts(values.astype(jnp.float32) - mean_ref[...])
        parts = []
        for tile in range(dim // TILE):
            here = slice(tile * TILE, (tile + 1) * TILE)
            upto = slice(0, (tile + 1) * TILE)
            part = product(high[:, upto], high_ref[here, upto], 1, 1)
            part += product(high[:, upto], low_ref[here, upto], 1, 1)
            part += product(low[:, upto], high_ref[here, upto], 1, 1)
            parts.append(part.astype(jnp.bfloat16))
        return jnp.concatenate(parts, axis=1)

    def lengths(white):
        wide = white.astype(jnp.float32)
        return lax.rsqrt(jnp.sum(wide * wide, axis=1, keepdims=True) + EPS)

    query = whitened(own_ref[...])
    query_norm = jnp.broadcast_to(lengths(query), (queries, queries)).T[0:1, :]
    density[...] = jnp.zeros_like(density)
    total[...] = jnp.zeros_like(total)

    def add_keys(start, step):
        block = keys[pl.ds(start, step), :]
        white = whitened(block)
        inner = product(white, query, 1, 1)
        scores = sharpness * (lengths(white) * query_norm * inner - 1.0)
        shape = (step, queries)
        key_index = start + lax.broadcasted_iota(jnp.int32, shape, 0)
        query_index = own_start + lax.broadcasted_iota(jnp.int32, shape, 1)
        seen = live_of(block) & (key_index != query_index)
        weights = jnp.where(seen, jnp.exp(scores), 0.0)
        density[...] += jnp.sum(weights, axis=0, keepdims=True)
        total[...] += product(weights.astype(jnp.bfloat16), white, 0, 0)

    over_chunks(rows, add_keys)
    dense = density[...]
    lane = lax.broadcasted_iota(jnp.int32, dense.shape, 1)
    logs = jnp.where(lane < own_size, jnp.log(dense), 0.0)
    divisor = jnp.broadcast_to(dense, (queries, queries)).T[:, 0:1]
    sublane = lax.broadcasted_iota(jnp.int32, (queries, 1), 0)
    means = jnp.where(sublane < own_size, total[...] / divisor, 0.0).astype(jnp.bfloat16)
    return logs, means


def local_kernel(group_count, size_ref, own_ref, *refs):
    groups, refs = refs[:group_count], refs[group_count:]
    log_ref, out_ref, keys, counts, sizes, starts, arrived, copied = refs[:8]
    mean_ref, work, found, block, part, high_ref, low_ref, density, total = refs[8:]
    rows, count = collect(groups, keys, counts, sizes, starts, arrived, copied)
    moments(keys, rows, count, mean_ref, work)
    whitener(work, found, block, part, high_ref, low_ref)
    block_count = size_ref.shape[0]
    block_rows = own_ref.shape[0] // block_count
    for here in range(block_count):
        span = slice(here * block_rows, (here + 1) * block_rows)
        log_ref[here : here + 1, :], out_ref[span, :] = scores(
            keys,
            rows,
            own_ref.at[span],
            size_ref[here],
            starts[here],
            mean_ref,
            high_ref,
            low_ref,
            density,
            total,
        )


def local_call(bucket_sizes, states, groups):
    row_count, dim = states.shape
    block_count = bucket_sizes.shape[0]
    block_rows = row_count // block_count
    key_rows = sum(group.shape[0] for group in groups)
    blocks = key_rows // LIVE_MAX
    square = (dim, dim)
    logs, means = pl.pallas_call(
        functools.partial(local_kernel, len(groups)),
        out_shape=[
            jax.ShapeDtypeStruct((block_count, block_rows), jnp.float32),
            jax.ShapeDtypeStruct((row_count, dim), jnp.bfloat16),
        ],
        in_specs=[
            pl.BlockSpec(memory_space=pltpu.SMEM),
            pl.BlockSpec(memory_space=pltpu.VMEM),
        ]
        + [pl.BlockSpec(memory_space=pl.ANY)] * len(groups),
        out_specs=[pl.BlockSpec(memory_space=pltpu.VMEM)] * 2,
        scratch_shapes=[
            pltpu.VMEM((key_rows, dim), jnp.bfloat16),
            pltpu.VMEM((blocks, LANES), jnp.int32),
            pltpu.SMEM((blocks, LANES), jnp.int32),
            pltpu.SMEM((blocks,), jnp.int32),
            pltpu.SemaphoreType.DMA((len(groups),)),
            pltpu.SemaphoreType.DMA,
            pltpu.VMEM((1, dim), jnp.float32),
            pltpu.VMEM(square, jnp.float32),
            pltpu.VMEM(square, jnp.float32),
            pltpu.VMEM((LANES, LANES), jnp.float32),
            pltpu.VMEM((LANES, LANES), jnp.float32),
            pltpu.VMEM(square, jnp.bfloat16),
            pltpu.VMEM(square, jnp.bfloat16),
            pltpu.VMEM((1, block_rows), jnp.float32),
            pltpu.VMEM((block_rows, dim), jnp.float32),
        ],
        compiler_params=pltpu.CompilerParams(vmem_limit_bytes=VMEM_BYTES),
    )(bucket_sizes, states, *groups)
    return logs.reshape(row_count), means


def shards(states, bucket_sizes):
    row_count, dim = states.shape
    block_count = bucket_sizes.shape[0]
    block_rows = row_count // block_count
    in_block = jnp.arange(LIVE_MAX, dtype=jnp.int32)
    own_live = (in_block[None, :] < bucket_sizes[:, None])[:, :, None]
    prefix = states.reshape(block_count, block_rows, dim)[:, :LIVE_MAX]
    sent = jnp.where(own_live, prefix, jnp.bfloat16(DEAD)).reshape(-1, dim)
    groups = gather_rows(sent)
    return local_call(bucket_sizes, states, groups)


def solution(mesh):
    placed = (P("dev", None), P("dev"))
    return jax.shard_map(
        shards, mesh=mesh, in_specs=placed, out_specs=(P("dev"), P("dev", None)), check_vma=False
    )
```

```python
import functools
import math

import jax
import jax.numpy as jnp
from jax import lax
from jax.experimental import pallas as pl
from jax.experimental.pallas import tpu as pltpu
from jax.sharding import PartitionSpec as P

EPS = 1e-06
RIDGE = 1.0
LIVE_MAX = 96
DEAD = 1024.0
DEAD_ABOVE = 512.0
SUB = 8
HALF = 8
LANES = 128
TILE = 256
PACK = 16
CHUNK = 512
REST = 256
VMEM_BYTES = 60 << 20
EXACT = lax.Precision.HIGHEST


def product(left, right, left_dim, right_dim, precision=None):
    return lax.dot_general(
        left,
        right,
        (((left_dim,), (right_dim,)), ((), ())),
        precision=precision,
        preferred_element_type=jnp.float32,
    )


def two_parts(value):
    high = value.astype(jnp.bfloat16)
    return high, (value - high.astype(jnp.float32)).astype(jnp.bfloat16)


def three_products(left, right):
    left_high, left_low = two_parts(left)
    right_high, right_low = two_parts(right)
    return (
        product(left_high, right_high, 1, 0)
        + product(left_high, right_low, 1, 0)
        + product(left_low, right_high, 1, 0)
    )


def flipped(value, mask):
    size = lax.axis_size("dev")
    return lax.ppermute(value, "dev", [(source, source ^ mask) for source in range(size)])


def plane_of(group, near, direct):
    if near != 8 or direct:
        return [group] + [flipped(group, mask) for mask in range(2, near, 2)]
    half = group.shape[0] // 2
    side, ahead = flipped(group, 2), flipped(group, 4)
    return [group, side, ahead, flipped(side[:half], 4), flipped(ahead[half:], 2)]


def gather_rows(rows):
    size = lax.axis_size("dev")
    near, far = size // 4, size // 2
    across, beside = flipped(rows, far), flipped(rows, near)
    groups = [rows, across, beside, flipped(across, near)]
    same_core = [
        jnp.concatenate(plane_of(group, near, place in (0, 3)), axis=0)
        for place, group in enumerate(groups)
    ]
    return same_core + [flipped(group, 1) for group in same_core]


def live_of(block):
    return block[:, :1].astype(jnp.float32) < DEAD_ABOVE


def over_chunks(rows, body):
    whole = (rows + (CHUNK - REST - 1)) // CHUNK

    @pl.loop(0, whole)
    def _(index):
        body(pl.multiple_of(index * CHUNK, CHUNK), CHUNK)

    @pl.when(whole * CHUNK < rows)
    def _():
        body(pl.multiple_of(whole * CHUNK, CHUNK), REST)


def collect(groups, keys, counts, sizes, starts, arrived, copied):
    blocks = keys.shape[0] // LIVE_MAX
    copies, first = [], 0
    for place, group in enumerate(groups):
        rows = group.shape[0]
        copies.append(
            pltpu.make_async_copy(group, keys.at[pl.ds(first, rows)], arrived.at[place])
        )
        copies[-1].start()
        first += rows
    first = 0
    for place, group in enumerate(groups):
        copies[place].wait()
        last = first + group.shape[0] // LIVE_MAX

        @pl.loop(first, last)
        def _(block):
            start = pl.multiple_of(block * LIVE_MAX, PACK)
            marks = keys[pl.ds(start, LIVE_MAX), :LANES].astype(jnp.float32)
            alive = jnp.sum((marks < DEAD_ABOVE).astype(jnp.float32), axis=0, keepdims=True)
            counts[pl.ds(block, 1), :] = alive.astype(jnp.int32)

        first = last
    copy = pltpu.make_async_copy(counts, sizes, copied)
    copy.start()
    copy.wait()

    def move_block(block, carry):
        offset, count = carry
        size = sizes[block, 0]
        tiles = (size + PACK - 1) // PACK
        starts[block] = offset

        def move_tile(tile, unused):
            source = pl.multiple_of(block * LIVE_MAX + tile * PACK, PACK)
            target = pl.multiple_of(offset + tile * PACK, PACK)
            keys[pl.ds(target, PACK), :] = keys[pl.ds(source, PACK), :]
            return unused

        lax.fori_loop(0, tiles, move_tile, 0)
        return offset + tiles * PACK, count + size

    rows, count = lax.fori_loop(0, blocks, move_block, (jnp.int32(0), jnp.int32(0)))

    @pl.loop(rows // PACK, pl.cdiv(rows, REST) * (REST // PACK))
    def _(tile):
        target = pl.multiple_of(tile * PACK, PACK)
        keys[pl.ds(target, PACK), :] = jnp.full((PACK, keys.shape[1]), DEAD, keys.dtype)

    return rows, count


def moments(keys, rows, count, mean_ref, work):
    dim = keys.shape[1]
    tiles = dim // TILE

    def add_sums(index, sums):
        start = pl.multiple_of(index * REST, REST)
        block = keys[pl.ds(start, REST), :]
        part = jnp.where(live_of(block), block.astype(jnp.float32), 0.0)
        return sums + jnp.sum(part.reshape(REST // SUB, SUB, dim), axis=0)

    sums = lax.fori_loop(0, pl.cdiv(rows, REST), add_sums, jnp.zeros((SUB, dim), jnp.float32))
    count = jnp.full((1, 1), count.astype(jnp.float32))
    mean = jnp.sum(sums, axis=0, keepdims=True) / count
    mean_ref[...] = mean
    work[...] = jnp.zeros_like(work)

    def add_products(start, step):
        block = keys[pl.ds(start, step), :]
        centred = jnp.where(live_of(block), block.astype(jnp.float32) - mean_ref[...], 0.0)
        high, low = two_parts(centred)
        for tile in range(tiles):
            here = slice(tile * TILE, (tile + 1) * TILE)
            upto = slice(0, (tile + 1) * TILE)
            part = product(high[:, here], high[:, upto], 0, 0)
            part += product(high[:, here], low[:, upto], 0, 0)
            part += product(low[:, here], high[:, upto], 0, 0)
            work[here, upto] += part

    over_chunks(rows, add_products)
    for tile in range(tiles):
        here = slice(tile * TILE, (tile + 1) * TILE)
        upto = slice(0, (tile + 1) * TILE)
        shape = (TILE, (tile + 1) * TILE)
        down = lax.broadcasted_iota(jnp.int32, shape, 0) + tile * TILE
        across = lax.broadcasted_iota(jnp.int32, shape, 1)
        work[here, upto] = work[here, upto] / count + jnp.where(down == across, RIDGE, 0.0)


def invert_factor(rows, inverse):
    count = len(rows)
    sublane = lax.broadcasted_iota(jnp.int32, (SUB, LANES), 0)

    def over_lanes(value, lane):
        return jnp.broadcast_to(value[:, lane : lane + 1], (SUB, LANES))

    def over_sublanes(value, row):
        return jnp.broadcast_to(value[row : row + 1, :], (SUB, LANES))

    upper = list(rows)
    for half in range(0, count, HALF):
        for step in range(half, half + HALF, 2):
            first = SUB * step
            pair = range(step, step + 2)
            columns = [[over_lanes(rows[v], first + t) for v in pair] for t in range(2 * SUB)]
            left, right = [rows[v] for v in pair], [inverse[v] for v in pair]
            done, solved = list(left), list(right)
            for t in range(2 * SUB):
                v, s = divmod(t, SUB)
                here = sublane == s
                pivot = over_sublanes(columns[t][v], s)
                root = lax.rsqrt(pivot)
                reciprocal = root * root
                factor = list(columns[t])
                factor[v] = jnp.where(here, -1.0, factor[v])

                def eliminate(values, raw):
                    scaled = raw * reciprocal
                    kept = list(values)
                    kept[v] = jnp.where(here, 0.0, kept[v])
                    return [k - f * scaled for k, f in zip(kept, factor)]

                for q in range(t + 1, 2 * SUB):
                    columns[q] = eliminate(columns[q], over_sublanes(columns[q][v], s))
                raw = over_sublanes(left[v], s)
                done[v] = jnp.where(here, raw * root, done[v])
                left = eliminate(left, raw)
                raw = over_sublanes(right[v], s)
                solved[v] = jnp.where(here, raw * root, solved[v])
                right = eliminate(right, raw)
            for v in range(2):
                upper[step + v], inverse[step + v] = done[v], solved[v]
            left = [over_sublanes(left[t // SUB], t % SUB) for t in range(2 * SUB)]
            right = [over_sublanes(right[t // SUB], t % SUB) for t in range(2 * SUB)]
            for i in range(step + 2, half + HALF):
                row, beside = rows[i], inverse[i]
                for t in range(2 * SUB):
                    column = over_lanes(rows[i], first + t)
                    row = row - column * left[t]
                    beside = beside - column * right[t]
                rows[i], inverse[i] = row, beside
        if half + HALF < count:
            span = slice(half, half + HALF)
            down = jnp.concatenate(upper[span], axis=0)
            across = jnp.concatenate([down, jnp.concatenate(inverse[span], axis=0)], axis=1)
            change = product(down, across, 0, 0, EXACT)
            for i in range(half + HALF, count):
                rows[i] = rows[i] - change[SUB * i : SUB * i + SUB, :LANES]
                inverse[i] = inverse[i] - change[SUB * i : SUB * i + SUB, LANES:]
    return inverse


def whitener(work, found, block, part, high_ref, low_ref):
    dim = work.shape[0]
    found[...] = jnp.zeros_like(found)
    block[...] = work[0:LANES, 0:LANES]
    count = LANES // SUB

    @pl.loop(0, dim // LANES)
    def _(index):
        lane = lax.broadcasted_iota(jnp.int32, (SUB, LANES), 1)
        sublane = lax.broadcasted_iota(jnp.int32, (SUB, LANES), 0)
        rows = [block[SUB * i : SUB * i + SUB, :] for i in range(count)]
        inverse = [(lane == sublane + SUB * i).astype(jnp.float32) for i in range(count)]
        inverse = invert_factor(rows, inverse)
        for i in range(count):
            part[SUB * i : SUB * i + SUB, :] = inverse[i]
        for here in range(dim // LANES):
            top = here // 2 * TILE
            mid, end = top + LANES, top + TILE

            @pl.when(index == here)
            def _(here=here, top=top, mid=mid, end=end):
                own = part[...]
                if here % 2 == 0:
                    left = product(work[mid:end, top:mid], own, 1, 1, EXACT)
                    block[...] = work[mid:end, mid:end] - product(left, left, 1, 1, EXACT)
                    found[top:mid, top:mid] = own
                    found[mid:end, top:mid] = product(left, own, 1, 0, EXACT)
                    return
                found[mid:end, mid:end] = own
                found[mid:end, top:mid] = -product(own, found[mid:end, top:mid], 1, 0, EXACT)
                pair = found[top:end, top:end]
                if end < dim:
                    panel = product(work[end:dim, top:end], pair, 1, 1, EXACT)
                    for low in range(0, dim - end, TILE):
                        size = low + TILE
                        strip = slice(end + low, end + size)
                        work[strip, end : end + size] = work[strip, end : end + size] - product(
                            panel[low:size], panel[0:size], 1, 1, EXACT
                        )
                    block[...] = work[end : end + LANES, end : end + LANES]
                if top > 0:
                    found[top:end, 0:top] = three_products(pair, found[top:end, 0:top])
                if end < dim:
                    found[end:dim, 0:end] = found[end:dim, 0:end] - three_products(
                        panel, found[top:end, 0:end]
                    )

    high, low = two_parts(found[...])
    high_ref[...] = high
    low_ref[...] = low


def scores(keys, rows, own_ref, own_size, own_start, mean_ref, high_ref, low_ref, density, total):
    dim = keys.shape[1]
    queries = own_ref.shape[0]
    sharpness = 2.0 * math.sqrt(dim)

    def whitened(values):
        high, low = two_parts(values.astype(jnp.float32) - mean_ref[...])
        parts = []
        for tile in range(dim // TILE):
            here = slice(tile * TILE, (tile + 1) * TILE)
            upto = slice(0, (tile + 1) * TILE)
            part = product(high[:, upto], high_ref[here, upto], 1, 1)
            part += product(high[:, upto], low_ref[here, upto], 1, 1)
            part += product(low[:, upto], high_ref[here, upto], 1, 1)
            parts.append(part.astype(jnp.bfloat16))
        return jnp.concatenate(parts, axis=1)

    def lengths(white):
        wide = white.astype(jnp.float32)
        return lax.rsqrt(jnp.sum(wide * wide, axis=1, keepdims=True) + EPS)

    query = whitened(own_ref[...])
    query_norm = jnp.broadcast_to(lengths(query), (queries, queries)).T[0:1, :]
    density[...] = jnp.zeros_like(density)
    total[...] = jnp.zeros_like(total)

    def add_keys(start, step):
        block = keys[pl.ds(start, step), :]
        white = whitened(block)
        inner = product(white, query, 1, 1)
        scores = sharpness * (lengths(white) * query_norm * inner - 1.0)
        shape = (step, queries)
        key_index = start + lax.broadcasted_iota(jnp.int32, shape, 0)
        query_index = own_start + lax.broadcasted_iota(jnp.int32, shape, 1)
        seen = live_of(block) & (key_index != query_index)
        weights = jnp.where(seen, jnp.exp(scores), 0.0)
        density[...] += jnp.sum(weights, axis=0, keepdims=True)
        total[...] += product(weights.astype(jnp.bfloat16), white, 0, 0)

    over_chunks(rows, add_keys)
    dense = density[...]
    lane = lax.broadcasted_iota(jnp.int32, dense.shape, 1)
    logs = jnp.where(lane < own_size, jnp.log(dense), 0.0)
    divisor = jnp.broadcast_to(dense, (queries, queries)).T[:, 0:1]
    sublane = lax.broadcasted_iota(jnp.int32, (queries, 1), 0)
    means = jnp.where(sublane < own_size, total[...] / divisor, 0.0).astype(jnp.bfloat16)
    return logs, means


def local_kernel(group_count, size_ref, own_ref, *refs):
    groups, refs = refs[:group_count], refs[group_count:]
    log_ref, out_ref, keys, counts, sizes, starts, arrived, copied = refs[:8]
    mean_ref, work, found, block, part, high_ref, low_ref, density, total = refs[8:]
    rows, count = collect(groups, keys, counts, sizes, starts, arrived, copied)
    moments(keys, rows, count, mean_ref, work)
    whitener(work, found, block, part, high_ref, low_ref)
    block_count = size_ref.shape[0]
    block_rows = own_ref.shape[0] // block_count
    for here in range(block_count):
        span = slice(here * block_rows, (here + 1) * block_rows)
        log_ref[here : here + 1, :], out_ref[span, :] = scores(
            keys,
            rows,
            own_ref.at[span],
            size_ref[here],
            starts[here],
            mean_ref,
            high_ref,
            low_ref,
            density,
            total,
        )


def local_call(bucket_sizes, states, groups):
    row_count, dim = states.shape
    block_count = bucket_sizes.shape[0]
    block_rows = row_count // block_count
    key_rows = sum(group.shape[0] for group in groups)
    blocks = key_rows // LIVE_MAX
    square = (dim, dim)
    logs, means = pl.pallas_call(
        functools.partial(local_kernel, len(groups)),
        out_shape=[
            jax.ShapeDtypeStruct((block_count, block_rows), jnp.float32),
            jax.ShapeDtypeStruct((row_count, dim), jnp.bfloat16),
        ],
        in_specs=[
            pl.BlockSpec(memory_space=pltpu.SMEM),
            pl.BlockSpec(memory_space=pltpu.VMEM),
        ]
        + [pl.BlockSpec(memory_space=pl.ANY)] * len(groups),
        out_specs=[pl.BlockSpec(memory_space=pltpu.VMEM)] * 2,
        scratch_shapes=[
            pltpu.VMEM((key_rows, dim), jnp.bfloat16),
            pltpu.VMEM((blocks, LANES), jnp.int32),
            pltpu.SMEM((blocks, LANES), jnp.int32),
            pltpu.SMEM((blocks,), jnp.int32),
            pltpu.SemaphoreType.DMA((len(groups),)),
            pltpu.SemaphoreType.DMA,
            pltpu.VMEM((1, dim), jnp.float32),
            pltpu.VMEM(square, jnp.float32),
            pltpu.VMEM(square, jnp.float32),
            pltpu.VMEM((LANES, LANES), jnp.float32),
            pltpu.VMEM((LANES, LANES), jnp.float32),
            pltpu.VMEM(square, jnp.bfloat16),
            pltpu.VMEM(square, jnp.bfloat16),
            pltpu.VMEM((1, block_rows), jnp.float32),
            pltpu.VMEM((block_rows, dim), jnp.float32),
        ],
        compiler_params=pltpu.CompilerParams(vmem_limit_bytes=VMEM_BYTES),
    )(bucket_sizes, states, *groups)
    return logs.reshape(row_count), means


def shards(states, bucket_sizes):
    row_count, dim = states.shape
    block_count = bucket_sizes.shape[0]
    block_rows = row_count // block_count
    in_block = jnp.arange(LIVE_MAX, dtype=jnp.int32)
    own_live = (in_block[None, :] < bucket_sizes[:, None])[:, :, None]
    prefix = states.reshape(block_count, block_rows, dim)[:, :LIVE_MAX]
    sent = jnp.where(own_live, prefix, jnp.bfloat16(DEAD)).reshape(-1, dim)
    groups = gather_rows(sent)
    return local_call(bucket_sizes, states, groups)


def solution(mesh):
    placed = (P("dev", None), P("dev"))
    return jax.shard_map(
        shards, mesh=mesh, in_specs=placed, out_specs=(P("dev"), P("dev", None)), check_vma=False
    )
```

```python
import functools
import math

import jax
import jax.numpy as jnp
from jax import lax
from jax.experimental import pallas as pl
from jax.experimental.pallas import tpu as pltpu
from jax.sharding import PartitionSpec as P

EPS = 1e-06
RIDGE = 1.0
LIVE_MAX = 96
DEAD = 1024.0
DEAD_ABOVE = 512.0
SUB = 8
HALF = 8
NEAR = 16.0
LANES = 128
TILE = 256
PACK = 16
CHUNK = 512
REST = 256
VMEM_BYTES = 60 << 20
EXACT = lax.Precision.HIGHEST


def product(left, right, left_dim, right_dim, precision=None):
    return lax.dot_general(
        left,
        right,
        (((left_dim,), (right_dim,)), ((), ())),
        precision=precision,
        preferred_element_type=jnp.float32,
    )


def two_parts(value):
    high = value.astype(jnp.bfloat16)
    return high, (value - high.astype(jnp.float32)).astype(jnp.bfloat16)


def three_products(left, right):
    left_high, left_low = two_parts(left)
    right_high, right_low = two_parts(right)
    return (
        product(left_high, right_high, 1, 0)
        + product(left_high, right_low, 1, 0)
        + product(left_low, right_high, 1, 0)
    )


def flipped(value, mask):
    size = lax.axis_size("dev")
    return lax.ppermute(value, "dev", [(source, source ^ mask) for source in range(size)])


def plane_of(group, near, direct):
    if near != 8 or direct:
        return [group] + [flipped(group, mask) for mask in range(2, near, 2)]
    half = group.shape[0] // 2
    side, ahead = flipped(group, 2), flipped(group, 4)
    return [group, side, ahead, flipped(side[:half], 4), flipped(ahead[half:], 2)]


def gather_rows(rows):
    size = lax.axis_size("dev")
    near, far = size // 4, size // 2
    across, beside = flipped(rows, far), flipped(rows, near)
    groups = [rows, across, beside, flipped(across, near)]
    same_core = [
        jnp.concatenate(plane_of(group, near, place in (0, 3)), axis=0)
        for place, group in enumerate(groups)
    ]
    return same_core + [flipped(group, 1) for group in same_core]


def live_of(block):
    return block[:, :1].astype(jnp.float32) < DEAD_ABOVE


def over_chunks(rows, body):
    whole = (rows + (CHUNK - REST - 1)) // CHUNK

    @pl.loop(0, whole)
    def _(index):
        body(pl.multiple_of(index * CHUNK, CHUNK), CHUNK)

    @pl.when(whole * CHUNK < rows)
    def _():
        body(pl.multiple_of(whole * CHUNK, CHUNK), REST)


def collect(groups, keys, counts, sizes, starts, arrived, copied):
    blocks = keys.shape[0] // LIVE_MAX
    copies, first = [], 0
    for place, group in enumerate(groups):
        rows = group.shape[0]
        copies.append(
            pltpu.make_async_copy(group, keys.at[pl.ds(first, rows)], arrived.at[place])
        )
        copies[-1].start()
        first += rows
    first = 0
    for place, group in enumerate(groups):
        copies[place].wait()
        last = first + group.shape[0] // LIVE_MAX

        @pl.loop(first, last)
        def _(block):
            start = pl.multiple_of(block * LIVE_MAX, PACK)
            marks = keys[pl.ds(start, LIVE_MAX), :LANES].astype(jnp.float32)
            alive = jnp.sum((marks < DEAD_ABOVE).astype(jnp.float32), axis=0, keepdims=True)
            counts[pl.ds(block, 1), :] = alive.astype(jnp.int32)

        first = last
    copy = pltpu.make_async_copy(counts, sizes, copied)
    copy.start()
    copy.wait()

    def move_block(block, carry):
        offset, count = carry
        size = sizes[block, 0]
        tiles = (size + PACK - 1) // PACK
        starts[block] = offset

        def move_tile(tile, unused):
            source = pl.multiple_of(block * LIVE_MAX + tile * PACK, PACK)
            target = pl.multiple_of(offset + tile * PACK, PACK)
            keys[pl.ds(target, PACK), :] = keys[pl.ds(source, PACK), :]
            return unused

        lax.fori_loop(0, tiles, move_tile, 0)
        return offset + tiles * PACK, count + size

    rows, count = lax.fori_loop(0, blocks, move_block, (jnp.int32(0), jnp.int32(0)))

    @pl.loop(rows // PACK, pl.cdiv(rows, REST) * (REST // PACK))
    def _(tile):
        target = pl.multiple_of(tile * PACK, PACK)
        keys[pl.ds(target, PACK), :] = jnp.full((PACK, keys.shape[1]), DEAD, keys.dtype)

    return rows, count


def moments(keys, rows, count, centre_ref, mean_ref, sums_ref, work):
    dim = keys.shape[1]
    spans = [
        (slice(tile * TILE, (tile + 1) * TILE), slice(0, (tile + 1) * TILE))
        for tile in range(dim // TILE)
    ]
    work[...] = jnp.zeros_like(work)
    sums_ref[...] = jnp.zeros_like(sums_ref)

    def add_plain(start, step):
        block = keys[pl.ds(start, step), :]
        live = live_of(block)
        high = jnp.where(live, block.astype(jnp.float32), 0.0).astype(block.dtype)
        alive = jnp.where(live, jnp.ones((step, LANES), jnp.float32), 0.0).astype(block.dtype)
        sums_ref[...] += product(alive, high, 0, 0)
        for here, upto in spans:
            work[here, upto] += product(high[:, here], high[:, upto], 0, 0)

    over_chunks(rows, add_plain)
    count = jnp.full((1, 1), count.astype(jnp.float32))
    mean = sums_ref[0:1, :] / count
    squares = []
    for here, upto in spans:
        shape = (TILE, TILE)
        down, across = (lax.broadcasted_iota(jnp.int32, shape, axis) for axis in (0, 1))
        diagonal = jnp.where(down == across, work[here, here], 0.0)
        squares.append(jnp.sum(diagonal, axis=0, keepdims=True))
    spread = jnp.concatenate(squares, axis=1) / count - mean * mean
    offset = jnp.max(jnp.where(mean * mean > NEAR * spread, 1.0, 0.0)) > 0.5
    centre_ref[...] = jnp.where(offset, mean, 0.0)
    mean_ref[...] = jnp.where(offset, 0.0, mean)

    @pl.when(offset)
    def _():
        work[...] = jnp.zeros_like(work)

        def add_centred(start, step):
            block = keys[pl.ds(start, step), :]
            centred = block.astype(jnp.float32) - centre_ref[...]
            high, low = two_parts(jnp.where(live_of(block), centred, 0.0))
            for here, upto in spans:
                part = product(high[:, here], high[:, upto], 0, 0)
                part += product(high[:, here], low[:, upto], 0, 0)
                part += product(low[:, here], high[:, upto], 0, 0)
                work[here, upto] += part

        over_chunks(rows, add_centred)

    for here, upto in spans:
        shape = (TILE, upto.stop)
        down = lax.broadcasted_iota(jnp.int32, shape, 0) + here.start
        across = lax.broadcasted_iota(jnp.int32, shape, 1)
        column = jnp.broadcast_to(mean_ref[:, here], (LANES, TILE)).T
        outer = jnp.concatenate([column] * (upto.stop // LANES), axis=1) * mean_ref[:, upto]
        ridge = jnp.where(down == across, RIDGE, 0.0)
        work[here, upto] = work[here, upto] / count - outer + ridge
    return offset


def invert_factor(rows, inverse):
    count = len(rows)
    sublane = lax.broadcasted_iota(jnp.int32, (SUB, LANES), 0)

    def over_lanes(value, lane):
        return jnp.broadcast_to(value[:, lane : lane + 1], (SUB, LANES))

    def over_sublanes(value, row):
        return jnp.broadcast_to(value[row : row + 1, :], (SUB, LANES))

    upper = list(rows)
    for half in range(0, count, HALF):
        for step in range(half, half + HALF, 2):
            first = SUB * step
            pair = range(step, step + 2)
            columns = [[over_lanes(rows[v], first + t) for v in pair] for t in range(2 * SUB)]
            left, right = [rows[v] for v in pair], [inverse[v] for v in pair]
            done, solved = list(left), list(right)
            for t in range(2 * SUB):
                v, s = divmod(t, SUB)
                here = sublane == s
                pivot = over_sublanes(columns[t][v], s)
                root = lax.rsqrt(pivot)
                reciprocal = root * root
                factor = list(columns[t])
                factor[v] = jnp.where(here, -1.0, factor[v])

                def eliminate(values, raw):
                    scaled = raw * reciprocal
                    kept = list(values)
                    kept[v] = jnp.where(here, 0.0, kept[v])
                    return [k - f * scaled for k, f in zip(kept, factor)]

                for q in range(t + 1, 2 * SUB):
                    columns[q] = eliminate(columns[q], over_sublanes(columns[q][v], s))
                raw = over_sublanes(left[v], s)
                done[v] = jnp.where(here, raw * root, done[v])
                left = eliminate(left, raw)
                raw = over_sublanes(right[v], s)
                solved[v] = jnp.where(here, raw * root, solved[v])
                right = eliminate(right, raw)
            for v in range(2):
                upper[step + v], inverse[step + v] = done[v], solved[v]
            left = [over_sublanes(left[t // SUB], t % SUB) for t in range(2 * SUB)]
            right = [over_sublanes(right[t // SUB], t % SUB) for t in range(2 * SUB)]
            for i in range(step + 2, half + HALF):
                row, beside = rows[i], inverse[i]
                for t in range(2 * SUB):
                    column = over_lanes(rows[i], first + t)
                    row = row - column * left[t]
                    beside = beside - column * right[t]
                rows[i], inverse[i] = row, beside
        if half + HALF < count:
            span = slice(half, half + HALF)
            down = jnp.concatenate(upper[span], axis=0)
            across = jnp.concatenate([down, jnp.concatenate(inverse[span], axis=0)], axis=1)
            change = product(down, across, 0, 0, EXACT)
            for i in range(half + HALF, count):
                rows[i] = rows[i] - change[SUB * i : SUB * i + SUB, :LANES]
                inverse[i] = inverse[i] - change[SUB * i : SUB * i + SUB, LANES:]
    return inverse


def whitener(work, found, block, part, high_ref, low_ref):
    dim = work.shape[0]
    found[...] = jnp.zeros_like(found)
    block[...] = work[0:LANES, 0:LANES]
    count = LANES // SUB

    @pl.loop(0, dim // LANES)
    def _(index):
        lane = lax.broadcasted_iota(jnp.int32, (SUB, LANES), 1)
        sublane = lax.broadcasted_iota(jnp.int32, (SUB, LANES), 0)
        rows = [block[SUB * i : SUB * i + SUB, :] for i in range(count)]
        inverse = [(lane == sublane + SUB * i).astype(jnp.float32) for i in range(count)]
        inverse = invert_factor(rows, inverse)
        for i in range(count):
            part[SUB * i : SUB * i + SUB, :] = inverse[i]
        for here in range(dim // LANES):
            top = here // 2 * TILE
            mid, end = top + LANES, top + TILE

            @pl.when(index == here)
            def _(here=here, top=top, mid=mid, end=end):
                own = part[...]
                if here % 2 == 0:
                    left = product(work[mid:end, top:mid], own, 1, 1, EXACT)
                    block[...] = work[mid:end, mid:end] - product(left, left, 1, 1, EXACT)
                    found[top:mid, top:mid] = own
                    found[mid:end, top:mid] = product(left, own, 1, 0, EXACT)
                    return
                found[mid:end, mid:end] = own
                found[mid:end, top:mid] = -product(own, found[mid:end, top:mid], 1, 0, EXACT)
                pair = found[top:end, top:end]
                if end < dim:
                    panel = product(work[end:dim, top:end], pair, 1, 1, EXACT)
                    for low in range(0, dim - end, TILE):
                        size = low + TILE
                        strip = slice(end + low, end + size)
                        work[strip, end : end + size] = work[strip, end : end + size] - product(
                            panel[low:size], panel[0:size], 1, 1, EXACT
                        )
                    block[...] = work[end : end + LANES, end : end + LANES]
                if top > 0:
                    found[top:end, 0:top] = three_products(pair, found[top:end, 0:top])
                if end < dim:
                    found[end:dim, 0:end] = found[end:dim, 0:end] - three_products(
                        panel, found[top:end, 0:end]
                    )

    high, low = two_parts(found[...])
    high_ref[...] = high
    low_ref[...] = low


def scores(
    keys,
    rows,
    offset,
    own_ref,
    own_size,
    own_start,
    centre_ref,
    mean_ref,
    high_ref,
    low_ref,
    white_ref,
    density,
    total,
):
    dim = keys.shape[1]
    queries = own_ref.shape[0]
    sharpness = 2.0 * math.sqrt(dim)
    mean_high, mean_low = two_parts(jnp.broadcast_to(mean_ref[...], (PACK, dim)))
    spans = [
        (slice(tile * TILE, (tile + 1) * TILE), slice(0, (tile + 1) * TILE))
        for tile in range(dim // TILE)
    ]
    moved = []
    for here, upto in spans:
        part = product(mean_high[:, upto], high_ref[here, upto], 1, 1)
        part += product(mean_high[:, upto], low_ref[here, upto], 1, 1)
        part += product(mean_low[:, upto], high_ref[here, upto], 1, 1)
        moved.append(part[0:1, :])

    def whitened(values):
        count = values.shape[0]

        @pl.when(offset)
        def _():
            high, low = two_parts(values.astype(jnp.float32) - centre_ref[...])
            for here, upto in spans:
                part = product(high[:, upto], high_ref[here, upto], 1, 1)
                part += product(high[:, upto], low_ref[here, upto], 1, 1)
                part += product(low[:, upto], high_ref[here, upto], 1, 1)
                white_ref[0:count, here] = part.astype(jnp.bfloat16)

        @pl.when(jnp.logical_not(offset))
        def _():
            for (here, upto), shift in zip(spans, moved):
                part = product(values[:, upto], high_ref[here, upto], 1, 1)
                part += product(values[:, upto], low_ref[here, upto], 1, 1)
                white_ref[0:count, here] = (part - shift).astype(jnp.bfloat16)

        return white_ref[0:count, :]

    def lengths(white):
        wide = white.astype(jnp.float32)
        return lax.rsqrt(jnp.sum(wide * wide, axis=1, keepdims=True) + EPS)

    query = whitened(own_ref[...])
    query_norm = jnp.broadcast_to(lengths(query), (queries, queries)).T[0:1, :]
    density[...] = jnp.zeros_like(density)
    total[...] = jnp.zeros_like(total)

    def add_keys(start, step):
        block = keys[pl.ds(start, step), :]
        white = whitened(block)
        inner = product(white, query, 1, 1)
        scores = sharpness * (lengths(white) * query_norm * inner - 1.0)
        shape = (step, queries)
        key_index = start + lax.broadcasted_iota(jnp.int32, shape, 0)
        query_index = own_start + lax.broadcasted_iota(jnp.int32, shape, 1)
        seen = live_of(block) & (key_index != query_index)
        weights = jnp.where(seen, jnp.exp(scores), 0.0)
        density[...] += jnp.sum(weights, axis=0, keepdims=True)
        total[...] += product(weights.astype(jnp.bfloat16), white, 0, 0)

    over_chunks(rows, add_keys)
    dense = density[...]
    lane = lax.broadcasted_iota(jnp.int32, dense.shape, 1)
    logs = jnp.where(lane < own_size, jnp.log(dense), 0.0)
    divisor = jnp.broadcast_to(dense, (queries, queries)).T[:, 0:1]
    sublane = lax.broadcasted_iota(jnp.int32, (queries, 1), 0)
    means = jnp.where(sublane < own_size, total[...] / divisor, 0.0).astype(jnp.bfloat16)
    return logs, means


def local_kernel(group_count, size_ref, own_ref, *refs):
    groups, refs = refs[:group_count], refs[group_count:]
    log_ref, out_ref, keys, counts, sizes, starts, arrived, copied = refs[:8]
    centre_ref, mean_ref, sums_ref, work, found, block, part, high_ref, low_ref = refs[8:17]
    white_ref, density, total = refs[17:]
    rows, count = collect(groups, keys, counts, sizes, starts, arrived, copied)
    offset = moments(keys, rows, count, centre_ref, mean_ref, sums_ref, work)
    whitener(work, found, block, part, high_ref, low_ref)
    block_count = size_ref.shape[0]
    block_rows = own_ref.shape[0] // block_count
    for here in range(block_count):
        span = slice(here * block_rows, (here + 1) * block_rows)
        log_ref[here : here + 1, :], out_ref[span, :] = scores(
            keys,
            rows,
            offset,
            own_ref.at[span],
            size_ref[here],
            starts[here],
            centre_ref,
            mean_ref,
            high_ref,
            low_ref,
            white_ref,
            density,
            total,
        )


def local_call(bucket_sizes, states, groups):
    row_count, dim = states.shape
    block_count = bucket_sizes.shape[0]
    block_rows = row_count // block_count
    key_rows = sum(group.shape[0] for group in groups)
    blocks = key_rows // LIVE_MAX
    square = (dim, dim)
    logs, means = pl.pallas_call(
        functools.partial(local_kernel, len(groups)),
        out_shape=[
            jax.ShapeDtypeStruct((block_count, block_rows), jnp.float32),
            jax.ShapeDtypeStruct((row_count, dim), jnp.bfloat16),
        ],
        in_specs=[
            pl.BlockSpec(memory_space=pltpu.SMEM),
            pl.BlockSpec(memory_space=pltpu.VMEM),
        ]
        + [pl.BlockSpec(memory_space=pl.ANY)] * len(groups),
        out_specs=[pl.BlockSpec(memory_space=pltpu.VMEM)] * 2,
        scratch_shapes=[
            pltpu.VMEM((key_rows, dim), jnp.bfloat16),
            pltpu.VMEM((blocks, LANES), jnp.int32),
            pltpu.SMEM((blocks, LANES), jnp.int32),
            pltpu.SMEM((blocks,), jnp.int32),
            pltpu.SemaphoreType.DMA((len(groups),)),
            pltpu.SemaphoreType.DMA,
            pltpu.VMEM((1, dim), jnp.float32),
            pltpu.VMEM((1, dim), jnp.float32),
            pltpu.VMEM((LANES, dim), jnp.float32),
            pltpu.VMEM(square, jnp.float32),
            pltpu.VMEM(square, jnp.float32),
            pltpu.VMEM((LANES, LANES), jnp.float32),
            pltpu.VMEM((LANES, LANES), jnp.float32),
            pltpu.VMEM(square, jnp.bfloat16),
            pltpu.VMEM(square, jnp.bfloat16),
            pltpu.VMEM((CHUNK, dim), jnp.bfloat16),
            pltpu.VMEM((1, block_rows), jnp.float32),
            pltpu.VMEM((block_rows, dim), jnp.float32),
        ],
        compiler_params=pltpu.CompilerParams(vmem_limit_bytes=VMEM_BYTES),
    )(bucket_sizes, states, *groups)
    return logs.reshape(row_count), means


def shards(states, bucket_sizes):
    row_count, dim = states.shape
    block_count = bucket_sizes.shape[0]
    block_rows = row_count // block_count
    in_block = jnp.arange(LIVE_MAX, dtype=jnp.int32)
    own_live = (in_block[None, :] < bucket_sizes[:, None])[:, :, None]
    prefix = states.reshape(block_count, block_rows, dim)[:, :LIVE_MAX]
    sent = jnp.where(own_live, prefix, jnp.bfloat16(DEAD)).reshape(-1, dim)
    groups = gather_rows(sent)
    return local_call(bucket_sizes, states, groups)


def solution(mesh):
    placed = (P("dev", None), P("dev"))
    return jax.shard_map(
        shards, mesh=mesh, in_specs=placed, out_specs=(P("dev"), P("dev", None)), check_vma=False
    )
```

```python
import functools
import math

import jax
import jax.numpy as jnp
from jax import lax
from jax.experimental import pallas as pl
from jax.experimental.pallas import tpu as pltpu
from jax.sharding import PartitionSpec as P

EPS = 1e-06
RIDGE = 1.0
LIVE_MAX = 96
DEAD = 1024.0
DEAD_ABOVE = 512.0
SUB = 8
HALF = 8
NEAR = 16.0
LANES = 128
TILE = 256
PACK = 16
CHUNK = 1024
REST = 256
VMEM_BYTES = 60 << 20
EXACT = lax.Precision.HIGHEST


def product(left, right, left_dim, right_dim, precision=None):
    return lax.dot_general(
        left,
        right,
        (((left_dim,), (right_dim,)), ((), ())),
        precision=precision,
        preferred_element_type=jnp.float32,
    )


def two_parts(value):
    high = value.astype(jnp.bfloat16)
    return high, (value - high.astype(jnp.float32)).astype(jnp.bfloat16)


def three_products(left, right):
    left_high, left_low = two_parts(left)
    right_high, right_low = two_parts(right)
    return (
        product(left_high, right_high, 1, 0)
        + product(left_high, right_low, 1, 0)
        + product(left_low, right_high, 1, 0)
    )


def flipped(value, mask):
    size = lax.axis_size("dev")
    return lax.ppermute(value, "dev", [(source, source ^ mask) for source in range(size)])


def plane_of(group, near, direct):
    if near != 8 or direct:
        return [group] + [flipped(group, mask) for mask in range(2, near, 2)]
    half = group.shape[0] // 2
    side, ahead = flipped(group, 2), flipped(group, 4)
    return [group, side, ahead, flipped(side[:half], 4), flipped(ahead[half:], 2)]


def gather_rows(rows):
    size = lax.axis_size("dev")
    near, far = size // 4, size // 2
    across, beside = flipped(rows, far), flipped(rows, near)
    groups = [rows, across, beside, flipped(across, near)]
    same_core = [
        jnp.concatenate(plane_of(group, near, place in (0, 3)), axis=0)
        for place, group in enumerate(groups)
    ]
    return same_core + [flipped(group, 1) for group in same_core]


def live_of(block):
    return block[:, :1].astype(jnp.float32) < DEAD_ABOVE


def chunk_plan(rows):
    parts = pl.cdiv(rows, REST)
    whole = (parts + 1) // (CHUNK // REST)
    return parts, whole, parts - whole * (CHUNK // REST)


def over_chunks(rows, body):
    _, whole, left = chunk_plan(rows)

    @pl.loop(0, whole)
    def _(index):
        body(pl.multiple_of(index * CHUNK, CHUNK), CHUNK)

    @pl.when(left == 2)
    def _():
        body(pl.multiple_of(whole * CHUNK, CHUNK), 2 * REST)

    @pl.when(left == 1)
    def _():
        body(pl.multiple_of(whole * CHUNK, CHUNK), REST)


def collect(groups, keys, counts, sizes, starts, arrived, copied):
    blocks = keys.shape[0] // LIVE_MAX
    copies, first = [], 0
    for place, group in enumerate(groups):
        rows = group.shape[0]
        copies.append(
            pltpu.make_async_copy(group, keys.at[pl.ds(first, rows)], arrived.at[place])
        )
        copies[-1].start()
        first += rows
    first = 0
    for place, group in enumerate(groups):
        copies[place].wait()
        last = first + group.shape[0] // LIVE_MAX

        @pl.loop(first, last)
        def _(block):
            start = pl.multiple_of(block * LIVE_MAX, PACK)
            marks = keys[pl.ds(start, LIVE_MAX), :LANES].astype(jnp.float32)
            alive = jnp.sum((marks < DEAD_ABOVE).astype(jnp.float32), axis=0, keepdims=True)
            counts[pl.ds(block, 1), :] = alive.astype(jnp.int32)

        first = last
    copy = pltpu.make_async_copy(counts, sizes, copied)
    copy.start()
    copy.wait()

    def move_block(block, carry):
        offset, count = carry
        size = sizes[block, 0]
        tiles = (size + PACK - 1) // PACK
        starts[block] = offset

        def move_tile(tile, unused):
            source = pl.multiple_of(block * LIVE_MAX + tile * PACK, PACK)
            target = pl.multiple_of(offset + tile * PACK, PACK)
            keys[pl.ds(target, PACK), :] = keys[pl.ds(source, PACK), :]
            return unused

        lax.fori_loop(0, tiles, move_tile, 0)
        return offset + tiles * PACK, count + size

    rows, count = lax.fori_loop(0, blocks, move_block, (jnp.int32(0), jnp.int32(0)))

    parts, whole, _ = chunk_plan(rows)
    filled = jnp.maximum(parts * REST, whole * CHUNK)

    @pl.loop(rows // PACK, filled // PACK)
    def _(tile):
        target = pl.multiple_of(tile * PACK, PACK)
        keys[pl.ds(target, PACK), :] = jnp.full((PACK, keys.shape[1]), DEAD, keys.dtype)

    return rows, count


def moments(keys, rows, count, centre_ref, mean_ref, sums_ref, work):
    dim = keys.shape[1]
    spans = [
        (slice(tile * TILE, (tile + 1) * TILE), slice(0, (tile + 1) * TILE))
        for tile in range(dim // TILE)
    ]
    work[...] = jnp.zeros_like(work)
    sums_ref[...] = jnp.zeros_like(sums_ref)

    def add_plain(start, step):
        block = keys[pl.ds(start, step), :]
        live = live_of(block)
        high = jnp.where(live, block.astype(jnp.float32), 0.0).astype(block.dtype)
        alive = jnp.where(live, jnp.ones((step, LANES), jnp.float32), 0.0).astype(block.dtype)
        sums_ref[...] += product(alive, high, 0, 0)
        for here, upto in spans:
            work[here, upto] += product(high[:, here], high[:, upto], 0, 0)

    over_chunks(rows, add_plain)
    count = jnp.full((1, 1), count.astype(jnp.float32))
    mean = sums_ref[0:1, :] / count
    squares = []
    for here, upto in spans:
        shape = (TILE, TILE)
        down, across = (lax.broadcasted_iota(jnp.int32, shape, axis) for axis in (0, 1))
        diagonal = jnp.where(down == across, work[here, here], 0.0)
        squares.append(jnp.sum(diagonal, axis=0, keepdims=True))
    spread = jnp.concatenate(squares, axis=1) / count - mean * mean
    offset = jnp.max(jnp.where(mean * mean > NEAR * spread, 1.0, 0.0)) > 0.5
    centre_ref[...] = jnp.where(offset, mean, 0.0)
    mean_ref[...] = jnp.where(offset, 0.0, mean)

    @pl.when(offset)
    def _():
        work[...] = jnp.zeros_like(work)

        def add_centred(start, step):
            block = keys[pl.ds(start, step), :]
            centred = block.astype(jnp.float32) - centre_ref[...]
            high, low = two_parts(jnp.where(live_of(block), centred, 0.0))
            for here, upto in spans:
                part = product(high[:, here], high[:, upto], 0, 0)
                part += product(high[:, here], low[:, upto], 0, 0)
                part += product(low[:, here], high[:, upto], 0, 0)
                work[here, upto] += part

        @pl.loop(0, pl.cdiv(rows, REST))
        def _(index):
            add_centred(pl.multiple_of(index * REST, REST), REST)

    for here, upto in spans:
        shape = (TILE, upto.stop)
        down = lax.broadcasted_iota(jnp.int32, shape, 0) + here.start
        across = lax.broadcasted_iota(jnp.int32, shape, 1)
        column = jnp.broadcast_to(mean_ref[:, here], (LANES, TILE)).T
        outer = jnp.concatenate([column] * (upto.stop // LANES), axis=1) * mean_ref[:, upto]
        ridge = jnp.where(down == across, RIDGE, 0.0)
        work[here, upto] = work[here, upto] / count - outer + ridge
    return offset


def invert_factor(rows, inverse):
    count = len(rows)
    sublane = lax.broadcasted_iota(jnp.int32, (SUB, LANES), 0)

    def over_lanes(value, lane):
        return jnp.broadcast_to(value[:, lane : lane + 1], (SUB, LANES))

    def over_sublanes(value, row):
        return jnp.broadcast_to(value[row : row + 1, :], (SUB, LANES))

    upper = list(rows)
    for half in range(0, count, HALF):
        for step in range(half, half + HALF, 2):
            first = SUB * step
            pair = range(step, step + 2)
            columns = [[over_lanes(rows[v], first + t) for v in pair] for t in range(2 * SUB)]
            left, right = [rows[v] for v in pair], [inverse[v] for v in pair]
            done, solved = list(left), list(right)
            for t in range(2 * SUB):
                v, s = divmod(t, SUB)
                here = sublane == s
                pivot = over_sublanes(columns[t][v], s)
                root = lax.rsqrt(pivot)
                reciprocal = root * root
                factor = list(columns[t])
                factor[v] = jnp.where(here, -1.0, factor[v])

                def eliminate(values, raw):
                    scaled = raw * reciprocal
                    kept = list(values)
                    kept[v] = jnp.where(here, 0.0, kept[v])
                    return [k - f * scaled for k, f in zip(kept, factor)]

                for q in range(t + 1, 2 * SUB):
                    columns[q] = eliminate(columns[q], over_sublanes(columns[q][v], s))
                raw = over_sublanes(left[v], s)
                done[v] = jnp.where(here, raw * root, done[v])
                left = eliminate(left, raw)
                raw = over_sublanes(right[v], s)
                solved[v] = jnp.where(here, raw * root, solved[v])
                right = eliminate(right, raw)
            for v in range(2):
                upper[step + v], inverse[step + v] = done[v], solved[v]
            left = [over_sublanes(left[t // SUB], t % SUB) for t in range(2 * SUB)]
            right = [over_sublanes(right[t // SUB], t % SUB) for t in range(2 * SUB)]
            for i in range(step + 2, half + HALF):
                row, beside = rows[i], inverse[i]
                for t in range(2 * SUB):
                    column = over_lanes(rows[i], first + t)
                    row = row - column * left[t]
                    beside = beside - column * right[t]
                rows[i], inverse[i] = row, beside
        if half + HALF < count:
            span = slice(half, half + HALF)
            down = jnp.concatenate(upper[span], axis=0)
            across = jnp.concatenate([down, jnp.concatenate(inverse[span], axis=0)], axis=1)
            change = product(down, across, 0, 0, EXACT)
            for i in range(half + HALF, count):
                rows[i] = rows[i] - change[SUB * i : SUB * i + SUB, :LANES]
                inverse[i] = inverse[i] - change[SUB * i : SUB * i + SUB, LANES:]
    return inverse


def whitener(work, found, block, part, high_ref, low_ref):
    dim = work.shape[0]
    found[...] = jnp.zeros_like(found)
    block[...] = work[0:LANES, 0:LANES]
    count = LANES // SUB

    @pl.loop(0, dim // LANES)
    def _(index):
        lane = lax.broadcasted_iota(jnp.int32, (SUB, LANES), 1)
        sublane = lax.broadcasted_iota(jnp.int32, (SUB, LANES), 0)
        rows = [block[SUB * i : SUB * i + SUB, :] for i in range(count)]
        inverse = [(lane == sublane + SUB * i).astype(jnp.float32) for i in range(count)]
        inverse = invert_factor(rows, inverse)
        for i in range(count):
            part[SUB * i : SUB * i + SUB, :] = inverse[i]
        for here in range(dim // LANES):
            top = here // 2 * TILE
            mid, end = top + LANES, top + TILE

            @pl.when(index == here)
            def _(here=here, top=top, mid=mid, end=end):
                own = part[...]
                if here % 2 == 0:
                    left = product(work[mid:end, top:mid], own, 1, 1, EXACT)
                    block[...] = work[mid:end, mid:end] - product(left, left, 1, 1, EXACT)
                    found[top:mid, top:mid] = own
                    found[mid:end, top:mid] = product(left, own, 1, 0, EXACT)
                    return
                found[mid:end, mid:end] = own
                found[mid:end, top:mid] = -product(own, found[mid:end, top:mid], 1, 0, EXACT)
                pair = found[top:end, top:end]
                if end < dim:
                    panel = product(work[end:dim, top:end], pair, 1, 1, EXACT)
                    for low in range(0, dim - end, TILE):
                        size = low + TILE
                        strip = slice(end + low, end + size)
                        work[strip, end : end + size] = work[strip, end : end + size] - product(
                            panel[low:size], panel[0:size], 1, 1, EXACT
                        )
                    block[...] = work[end : end + LANES, end : end + LANES]
                if top > 0:
                    found[top:end, 0:top] = three_products(pair, found[top:end, 0:top])
                if end < dim:
                    found[end:dim, 0:end] = found[end:dim, 0:end] - three_products(
                        panel, found[top:end, 0:end]
                    )

    high, low = two_parts(found[...])
    high_ref[...] = high
    low_ref[...] = low


def scores(
    keys,
    rows,
    offset,
    own_ref,
    own_size,
    own_start,
    centre_ref,
    mean_ref,
    high_ref,
    low_ref,
    white_ref,
    density,
    total,
):
    dim = keys.shape[1]
    queries = own_ref.shape[0]
    sharpness = 2.0 * math.sqrt(dim)
    mean_high, mean_low = two_parts(jnp.broadcast_to(mean_ref[...], (PACK, dim)))
    spans = [
        (slice(tile * TILE, (tile + 1) * TILE), slice(0, (tile + 1) * TILE))
        for tile in range(dim // TILE)
    ]
    moved = []
    for here, upto in spans:
        part = product(mean_high[:, upto], high_ref[here, upto], 1, 1)
        part += product(mean_high[:, upto], low_ref[here, upto], 1, 1)
        part += product(mean_low[:, upto], high_ref[here, upto], 1, 1)
        moved.append(part[0:1, :])

    def whitened(values):
        count = values.shape[0]

        @pl.when(offset)
        def _():
            high, low = two_parts(values.astype(jnp.float32) - centre_ref[...])
            for here, upto in spans:
                part = product(high[:, upto], high_ref[here, upto], 1, 1)
                part += product(high[:, upto], low_ref[here, upto], 1, 1)
                part += product(low[:, upto], high_ref[here, upto], 1, 1)
                white_ref[0:count, here] = part.astype(jnp.bfloat16)

        @pl.when(jnp.logical_not(offset))
        def _():
            for (here, upto), shift in zip(spans, moved):
                part = product(values[:, upto], high_ref[here, upto], 1, 1)
                part += product(values[:, upto], low_ref[here, upto], 1, 1)
                white_ref[0:count, here] = (part - shift).astype(jnp.bfloat16)

        return white_ref[0:count, :]

    def lengths(white):
        wide = white.astype(jnp.float32)
        return lax.rsqrt(jnp.sum(wide * wide, axis=1, keepdims=True) + EPS)

    query = whitened(own_ref[...])
    query_norm = jnp.broadcast_to(lengths(query), (queries, queries)).T[0:1, :]
    density[...] = jnp.zeros_like(density)
    total[...] = jnp.zeros_like(total)

    def add_keys(start, step):
        block = keys[pl.ds(start, step), :]
        white = whitened(block)
        inner = product(white, query, 1, 1)
        scores = sharpness * (lengths(white) * query_norm * inner - 1.0)
        shape = (step, queries)
        key_index = start + lax.broadcasted_iota(jnp.int32, shape, 0)
        query_index = own_start + lax.broadcasted_iota(jnp.int32, shape, 1)
        seen = live_of(block) & (key_index != query_index)
        weights = jnp.where(seen, jnp.exp(scores), 0.0)
        density[...] += jnp.sum(weights, axis=0, keepdims=True)
        total[...] += product(weights.astype(jnp.bfloat16), white, 0, 0)

    over_chunks(rows, add_keys)
    dense = density[...]
    lane = lax.broadcasted_iota(jnp.int32, dense.shape, 1)
    logs = jnp.where(lane < own_size, jnp.log(dense), 0.0)
    divisor = jnp.broadcast_to(dense, (queries, queries)).T[:, 0:1]
    sublane = lax.broadcasted_iota(jnp.int32, (queries, 1), 0)
    means = jnp.where(sublane < own_size, total[...] / divisor, 0.0).astype(jnp.bfloat16)
    return logs, means


def local_kernel(group_count, size_ref, own_ref, *refs):
    groups, refs = refs[:group_count], refs[group_count:]
    log_ref, out_ref, keys, counts, sizes, starts, arrived, copied = refs[:8]
    centre_ref, mean_ref, sums_ref, work, found, block, part, high_ref, low_ref = refs[8:17]
    white_ref, density, total = refs[17:]
    rows, count = collect(groups, keys, counts, sizes, starts, arrived, copied)
    offset = moments(keys, rows, count, centre_ref, mean_ref, sums_ref, work)
    whitener(work, found, block, part, high_ref, low_ref)
    block_count = size_ref.shape[0]
    block_rows = own_ref.shape[0] // block_count
    for here in range(block_count):
        span = slice(here * block_rows, (here + 1) * block_rows)
        log_ref[here : here + 1, :], out_ref[span, :] = scores(
            keys,
            rows,
            offset,
            own_ref.at[span],
            size_ref[here],
            starts[here],
            centre_ref,
            mean_ref,
            high_ref,
            low_ref,
            white_ref,
            density,
            total,
        )


def local_call(bucket_sizes, states, groups):
    row_count, dim = states.shape
    block_count = bucket_sizes.shape[0]
    block_rows = row_count // block_count
    key_rows = sum(group.shape[0] for group in groups)
    blocks = key_rows // LIVE_MAX
    square = (dim, dim)
    logs, means = pl.pallas_call(
        functools.partial(local_kernel, len(groups)),
        out_shape=[
            jax.ShapeDtypeStruct((block_count, block_rows), jnp.float32),
            jax.ShapeDtypeStruct((row_count, dim), jnp.bfloat16),
        ],
        in_specs=[
            pl.BlockSpec(memory_space=pltpu.SMEM),
            pl.BlockSpec(memory_space=pltpu.VMEM),
        ]
        + [pl.BlockSpec(memory_space=pl.ANY)] * len(groups),
        out_specs=[pl.BlockSpec(memory_space=pltpu.VMEM)] * 2,
        scratch_shapes=[
            pltpu.VMEM((key_rows, dim), jnp.bfloat16),
            pltpu.VMEM((blocks, LANES), jnp.int32),
            pltpu.SMEM((blocks, LANES), jnp.int32),
            pltpu.SMEM((blocks,), jnp.int32),
            pltpu.SemaphoreType.DMA((len(groups),)),
            pltpu.SemaphoreType.DMA,
            pltpu.VMEM((1, dim), jnp.float32),
            pltpu.VMEM((1, dim), jnp.float32),
            pltpu.VMEM((LANES, dim), jnp.float32),
            pltpu.VMEM(square, jnp.float32),
            pltpu.VMEM(square, jnp.float32),
            pltpu.VMEM((LANES, LANES), jnp.float32),
            pltpu.VMEM((LANES, LANES), jnp.float32),
            pltpu.VMEM(square, jnp.bfloat16),
            pltpu.VMEM(square, jnp.bfloat16),
            pltpu.VMEM((CHUNK, dim), jnp.bfloat16),
            pltpu.VMEM((1, block_rows), jnp.float32),
            pltpu.VMEM((block_rows, dim), jnp.float32),
        ],
        compiler_params=pltpu.CompilerParams(vmem_limit_bytes=VMEM_BYTES),
    )(bucket_sizes, states, *groups)
    return logs.reshape(row_count), means


def shards(states, bucket_sizes):
    row_count, dim = states.shape
    block_count = bucket_sizes.shape[0]
    block_rows = row_count // block_count
    in_block = jnp.arange(LIVE_MAX, dtype=jnp.int32)
    own_live = (in_block[None, :] < bucket_sizes[:, None])[:, :, None]
    prefix = states.reshape(block_count, block_rows, dim)[:, :LIVE_MAX]
    sent = jnp.where(own_live, prefix, jnp.bfloat16(DEAD)).reshape(-1, dim)
    groups = gather_rows(sent)
    return local_call(bucket_sizes, states, groups)


def solution(mesh):
    placed = (P("dev", None), P("dev"))
    return jax.shard_map(
        shards, mesh=mesh, in_specs=placed, out_specs=(P("dev"), P("dev", None)), check_vma=False
    )
```

```python
import functools
import math

import jax
import jax.numpy as jnp
from jax import lax
from jax.experimental import pallas as pl
from jax.experimental.pallas import tpu as pltpu
from jax.sharding import PartitionSpec as P

EPS = 1e-06
RIDGE = 1.0
LIVE_MAX = 96
DEAD = 1024.0
DEAD_ABOVE = 512.0
SUB = 8
HALF = 8
NEAR = 16.0
LANES = 128
TILE = 256
PACK = 16
CHUNK = 1024
REST = 256
VMEM_BYTES = 60 << 20
EXACT = lax.Precision.HIGHEST


def product(left, right, left_dim, right_dim, precision=None):
    return lax.dot_general(
        left,
        right,
        (((left_dim,), (right_dim,)), ((), ())),
        precision=precision,
        preferred_element_type=jnp.float32,
    )


def two_parts(value):
    high = value.astype(jnp.bfloat16)
    return high, (value - high.astype(jnp.float32)).astype(jnp.bfloat16)


def three_products(left, right):
    left_high, left_low = two_parts(left)
    right_high, right_low = two_parts(right)
    return (
        product(left_high, right_high, 1, 0)
        + product(left_high, right_low, 1, 0)
        + product(left_low, right_high, 1, 0)
    )


def flipped(value, mask):
    size = lax.axis_size("dev")
    return lax.ppermute(value, "dev", [(source, source ^ mask) for source in range(size)])


def plane_of(group, near, direct):
    if near != 8 or direct:
        return [group] + [flipped(group, mask) for mask in range(2, near, 2)]
    half = group.shape[0] // 2
    side, ahead = flipped(group, 2), flipped(group, 4)
    return [group, side, ahead, flipped(side[:half], 4), flipped(ahead[half:], 2)]


def gather_rows(rows):
    size = lax.axis_size("dev")
    near, far = size // 4, size // 2
    across, beside = flipped(rows, far), flipped(rows, near)
    groups = [rows, across, beside, flipped(across, near)]
    same_core = [
        jnp.concatenate(plane_of(group, near, place == 0), axis=0)
        for place, group in enumerate(groups[:3])
    ]
    same_core += plane_of(groups[3], near, True)
    return same_core + [flipped(group, 1) for group in same_core]


def live_of(block):
    return block[:, :1].astype(jnp.float32) < DEAD_ABOVE


def chunk_plan(rows):
    parts = pl.cdiv(rows, REST)
    whole = (parts + 1) // (CHUNK // REST)
    return parts, whole, parts - whole * (CHUNK // REST)


def over_chunks(rows, body):
    _, whole, left = chunk_plan(rows)

    @pl.loop(0, whole)
    def _(index):
        body(pl.multiple_of(index * CHUNK, CHUNK), CHUNK)

    @pl.when(left == 2)
    def _():
        body(pl.multiple_of(whole * CHUNK, CHUNK), 2 * REST)

    @pl.when(left == 1)
    def _():
        body(pl.multiple_of(whole * CHUNK, CHUNK), REST)


def collect(groups, keys, counts, sizes, starts, arrived, copied):
    blocks = keys.shape[0] // LIVE_MAX
    copies, first = [], 0
    for place, group in enumerate(groups):
        rows = group.shape[0]
        copies.append(
            pltpu.make_async_copy(group, keys.at[pl.ds(first, rows)], arrived.at[place])
        )
        copies[-1].start()
        first += rows
    first = 0
    for place, group in enumerate(groups):
        copies[place].wait()
        last = first + group.shape[0] // LIVE_MAX

        @pl.loop(first, last)
        def _(block):
            start = pl.multiple_of(block * LIVE_MAX, PACK)
            marks = keys[pl.ds(start, LIVE_MAX), :LANES].astype(jnp.float32)
            alive = jnp.sum((marks < DEAD_ABOVE).astype(jnp.float32), axis=0, keepdims=True)
            counts[pl.ds(block, 1), :] = alive.astype(jnp.int32)

        first = last
    copy = pltpu.make_async_copy(counts, sizes, copied)
    copy.start()
    copy.wait()

    def move_block(block, carry):
        offset, count = carry
        size = sizes[block, 0]
        tiles = (size + PACK - 1) // PACK
        starts[block] = offset

        def move_tile(tile, unused):
            source = pl.multiple_of(block * LIVE_MAX + tile * PACK, PACK)
            target = pl.multiple_of(offset + tile * PACK, PACK)
            keys[pl.ds(target, PACK), :] = keys[pl.ds(source, PACK), :]
            return unused

        lax.fori_loop(0, tiles, move_tile, 0)
        return offset + tiles * PACK, count + size

    rows, count = lax.fori_loop(0, blocks, move_block, (jnp.int32(0), jnp.int32(0)))

    parts, whole, _ = chunk_plan(rows)
    filled = jnp.maximum(parts * REST, whole * CHUNK)

    @pl.loop(rows // PACK, filled // PACK)
    def _(tile):
        target = pl.multiple_of(tile * PACK, PACK)
        keys[pl.ds(target, PACK), :] = jnp.full((PACK, keys.shape[1]), DEAD, keys.dtype)

    return rows, count


def moments(keys, rows, count, centre_ref, mean_ref, sums_ref, work):
    dim = keys.shape[1]
    spans = [
        (slice(tile * TILE, (tile + 1) * TILE), slice(0, (tile + 1) * TILE))
        for tile in range(dim // TILE)
    ]
    work[...] = jnp.zeros_like(work)
    sums_ref[...] = jnp.zeros_like(sums_ref)

    def add_plain(start, step):
        block = keys[pl.ds(start, step), :]
        live = live_of(block)
        high = jnp.where(live, block.astype(jnp.float32), 0.0).astype(block.dtype)
        alive = jnp.where(live, jnp.ones((step, LANES), jnp.float32), 0.0).astype(block.dtype)
        sums_ref[...] += product(alive, high, 0, 0)
        for here, upto in spans:
            work[here, upto] += product(high[:, here], high[:, upto], 0, 0)

    over_chunks(rows, add_plain)
    count = jnp.full((1, 1), count.astype(jnp.float32))
    mean = sums_ref[0:1, :] / count
    squares = []
    for here, upto in spans:
        shape = (TILE, TILE)
        down, across = (lax.broadcasted_iota(jnp.int32, shape, axis) for axis in (0, 1))
        diagonal = jnp.where(down == across, work[here, here], 0.0)
        squares.append(jnp.sum(diagonal, axis=0, keepdims=True))
    spread = jnp.concatenate(squares, axis=1) / count - mean * mean
    offset = jnp.max(jnp.where(mean * mean > NEAR * spread, 1.0, 0.0)) > 0.5
    centre_ref[...] = jnp.where(offset, mean, 0.0)
    mean_ref[...] = jnp.where(offset, 0.0, mean)

    @pl.when(offset)
    def _():
        work[...] = jnp.zeros_like(work)

        def add_centred(start, step):
            block = keys[pl.ds(start, step), :]
            centred = block.astype(jnp.float32) - centre_ref[...]
            high, low = two_parts(jnp.where(live_of(block), centred, 0.0))
            for here, upto in spans:
                part = product(high[:, here], high[:, upto], 0, 0)
                part += product(high[:, here], low[:, upto], 0, 0)
                part += product(low[:, here], high[:, upto], 0, 0)
                work[here, upto] += part

        @pl.loop(0, pl.cdiv(rows, REST))
        def _(index):
            add_centred(pl.multiple_of(index * REST, REST), REST)

    for here, upto in spans:
        shape = (TILE, upto.stop)
        down = lax.broadcasted_iota(jnp.int32, shape, 0) + here.start
        across = lax.broadcasted_iota(jnp.int32, shape, 1)
        column = jnp.broadcast_to(mean_ref[:, here], (LANES, TILE)).T
        outer = jnp.concatenate([column] * (upto.stop // LANES), axis=1) * mean_ref[:, upto]
        ridge = jnp.where(down == across, RIDGE, 0.0)
        work[here, upto] = work[here, upto] / count - outer + ridge
    return offset


def invert_factor(rows, inverse):
    count = len(rows)
    sublane = lax.broadcasted_iota(jnp.int32, (SUB, LANES), 0)

    def over_lanes(value, lane):
        return jnp.broadcast_to(value[:, lane : lane + 1], (SUB, LANES))

    def over_sublanes(value, row):
        return jnp.broadcast_to(value[row : row + 1, :], (SUB, LANES))

    upper = list(rows)
    for half in range(0, count, HALF):
        for step in range(half, half + HALF, 2):
            first = SUB * step
            pair = range(step, step + 2)
            columns = [[over_lanes(rows[v], first + t) for v in pair] for t in range(2 * SUB)]
            left, right = [rows[v] for v in pair], [inverse[v] for v in pair]
            done, solved = list(left), list(right)
            for t in range(2 * SUB):
                v, s = divmod(t, SUB)
                here = sublane == s
                pivot = over_sublanes(columns[t][v], s)
                root = lax.rsqrt(pivot)
                reciprocal = root * root
                factor = list(columns[t])
                factor[v] = jnp.where(here, -1.0, factor[v])

                def eliminate(values, raw):
                    scaled = raw * reciprocal
                    kept = list(values)
                    kept[v] = jnp.where(here, 0.0, kept[v])
                    return [k - f * scaled for k, f in zip(kept, factor)]

                for q in range(t + 1, 2 * SUB):
                    columns[q] = eliminate(columns[q], over_sublanes(columns[q][v], s))
                raw = over_sublanes(left[v], s)
                done[v] = jnp.where(here, raw * root, done[v])
                left = eliminate(left, raw)
                raw = over_sublanes(right[v], s)
                solved[v] = jnp.where(here, raw * root, solved[v])
                right = eliminate(right, raw)
            for v in range(2):
                upper[step + v], inverse[step + v] = done[v], solved[v]
            left = [over_sublanes(left[t // SUB], t % SUB) for t in range(2 * SUB)]
            right = [over_sublanes(right[t // SUB], t % SUB) for t in range(2 * SUB)]
            for i in range(step + 2, half + HALF):
                row, beside = rows[i], inverse[i]
                for t in range(2 * SUB):
                    column = over_lanes(rows[i], first + t)
                    row = row - column * left[t]
                    beside = beside - column * right[t]
                rows[i], inverse[i] = row, beside
        if half + HALF < count:
            span = slice(half, half + HALF)
            down = jnp.concatenate(upper[span], axis=0)
            across = jnp.concatenate([down, jnp.concatenate(inverse[span], axis=0)], axis=1)
            change = product(down, across, 0, 0, EXACT)
            for i in range(half + HALF, count):
                rows[i] = rows[i] - change[SUB * i : SUB * i + SUB, :LANES]
                inverse[i] = inverse[i] - change[SUB * i : SUB * i + SUB, LANES:]
    return inverse


def whitener(work, found, block, part, high_ref, low_ref):
    dim = work.shape[0]
    found[...] = jnp.zeros_like(found)
    block[...] = work[0:LANES, 0:LANES]
    count = LANES // SUB

    @pl.loop(0, dim // LANES)
    def _(index):
        lane = lax.broadcasted_iota(jnp.int32, (SUB, LANES), 1)
        sublane = lax.broadcasted_iota(jnp.int32, (SUB, LANES), 0)
        rows = [block[SUB * i : SUB * i + SUB, :] for i in range(count)]
        inverse = [(lane == sublane + SUB * i).astype(jnp.float32) for i in range(count)]
        inverse = invert_factor(rows, inverse)
        for i in range(count):
            part[SUB * i : SUB * i + SUB, :] = inverse[i]
        for here in range(dim // LANES):
            top = here // 2 * TILE
            mid, end = top + LANES, top + TILE

            @pl.when(index == here)
            def _(here=here, top=top, mid=mid, end=end):
                own = part[...]
                if here % 2 == 0:
                    left = product(work[mid:end, top:mid], own, 1, 1, EXACT)
                    block[...] = work[mid:end, mid:end] - product(left, left, 1, 1, EXACT)
                    found[top:mid, top:mid] = own
                    found[mid:end, top:mid] = product(left, own, 1, 0, EXACT)
                    return
                found[mid:end, mid:end] = own
                found[mid:end, top:mid] = -product(own, found[mid:end, top:mid], 1, 0, EXACT)
                pair = found[top:end, top:end]
                if end < dim:
                    panel = product(work[end:dim, top:end], pair, 1, 1, EXACT)
                    for low in range(0, dim - end, TILE):
                        size = low + TILE
                        strip = slice(end + low, end + size)
                        work[strip, end : end + size] = work[strip, end : end + size] - product(
                            panel[low:size], panel[0:size], 1, 1, EXACT
                        )
                    block[...] = work[end : end + LANES, end : end + LANES]
                if top > 0:
                    found[top:end, 0:top] = three_products(pair, found[top:end, 0:top])
                if end < dim:
                    found[end:dim, 0:end] = found[end:dim, 0:end] - three_products(
                        panel, found[top:end, 0:end]
                    )

    high, low = two_parts(found[...])
    high_ref[...] = high
    low_ref[...] = low


def scores(
    keys,
    rows,
    offset,
    own_ref,
    own_size,
    own_start,
    centre_ref,
    mean_ref,
    high_ref,
    low_ref,
    white_ref,
    density,
    total,
):
    dim = keys.shape[1]
    queries = own_ref.shape[0]
    sharpness = 2.0 * math.sqrt(dim)
    mean_high, mean_low = two_parts(jnp.broadcast_to(mean_ref[...], (PACK, dim)))
    spans = [
        (slice(tile * TILE, (tile + 1) * TILE), slice(0, (tile + 1) * TILE))
        for tile in range(dim // TILE)
    ]
    moved = []
    for here, upto in spans:
        part = product(mean_high[:, upto], high_ref[here, upto], 1, 1)
        part += product(mean_high[:, upto], low_ref[here, upto], 1, 1)
        part += product(mean_low[:, upto], high_ref[here, upto], 1, 1)
        moved.append(part[0:1, :])

    def whitened(values):
        count = values.shape[0]

        @pl.when(offset)
        def _():
            high, low = two_parts(values.astype(jnp.float32) - centre_ref[...])
            for here, upto in spans:
                part = product(high[:, upto], high_ref[here, upto], 1, 1)
                part += product(high[:, upto], low_ref[here, upto], 1, 1)
                part += product(low[:, upto], high_ref[here, upto], 1, 1)
                white_ref[0:count, here] = part.astype(jnp.bfloat16)

        @pl.when(jnp.logical_not(offset))
        def _():
            for (here, upto), shift in zip(spans, moved):
                part = product(values[:, upto], high_ref[here, upto], 1, 1)
                part += product(values[:, upto], low_ref[here, upto], 1, 1)
                white_ref[0:count, here] = (part - shift).astype(jnp.bfloat16)

        return white_ref[0:count, :]

    def lengths(white):
        wide = white.astype(jnp.float32)
        return lax.rsqrt(jnp.sum(wide * wide, axis=1, keepdims=True) + EPS)

    query = whitened(own_ref[...])
    query_norm = jnp.broadcast_to(lengths(query), (queries, queries)).T[0:1, :]
    density[...] = jnp.zeros_like(density)
    total[...] = jnp.zeros_like(total)

    def add_keys(start, step):
        block = keys[pl.ds(start, step), :]
        white = whitened(block)
        inner = product(white, query, 1, 1)
        scores = sharpness * (lengths(white) * query_norm * inner - 1.0)
        shape = (step, queries)
        key_index = start + lax.broadcasted_iota(jnp.int32, shape, 0)
        query_index = own_start + lax.broadcasted_iota(jnp.int32, shape, 1)
        seen = live_of(block) & (key_index != query_index)
        weights = jnp.where(seen, jnp.exp(scores), 0.0)
        density[...] += jnp.sum(weights, axis=0, keepdims=True)
        total[...] += product(weights.astype(jnp.bfloat16), white, 0, 0)

    over_chunks(rows, add_keys)
    dense = density[...]
    lane = lax.broadcasted_iota(jnp.int32, dense.shape, 1)
    logs = jnp.where(lane < own_size, jnp.log(dense), 0.0)
    divisor = jnp.broadcast_to(dense, (queries, queries)).T[:, 0:1]
    sublane = lax.broadcasted_iota(jnp.int32, (queries, 1), 0)
    means = jnp.where(sublane < own_size, total[...] / divisor, 0.0).astype(jnp.bfloat16)
    return logs, means


def local_kernel(group_count, size_ref, own_ref, *refs):
    groups, refs = refs[:group_count], refs[group_count:]
    log_ref, out_ref, keys, counts, sizes, starts, arrived, copied = refs[:8]
    centre_ref, mean_ref, sums_ref, work, found, block, part, high_ref, low_ref = refs[8:17]
    white_ref, density, total = refs[17:]
    rows, count = collect(groups, keys, counts, sizes, starts, arrived, copied)
    offset = moments(keys, rows, count, centre_ref, mean_ref, sums_ref, work)
    whitener(work, found, block, part, high_ref, low_ref)
    block_count = size_ref.shape[0]
    block_rows = own_ref.shape[0] // block_count
    for here in range(block_count):
        span = slice(here * block_rows, (here + 1) * block_rows)
        log_ref[here : here + 1, :], out_ref[span, :] = scores(
            keys,
            rows,
            offset,
            own_ref.at[span],
            size_ref[here],
            starts[here],
            centre_ref,
            mean_ref,
            high_ref,
            low_ref,
            white_ref,
            density,
            total,
        )


def local_call(bucket_sizes, states, groups):
    row_count, dim = states.shape
    block_count = bucket_sizes.shape[0]
    block_rows = row_count // block_count
    key_rows = sum(group.shape[0] for group in groups)
    blocks = key_rows // LIVE_MAX
    square = (dim, dim)
    logs, means = pl.pallas_call(
        functools.partial(local_kernel, len(groups)),
        out_shape=[
            jax.ShapeDtypeStruct((block_count, block_rows), jnp.float32),
            jax.ShapeDtypeStruct((row_count, dim), jnp.bfloat16),
        ],
        in_specs=[
            pl.BlockSpec(memory_space=pltpu.SMEM),
            pl.BlockSpec(memory_space=pltpu.VMEM),
        ]
        + [pl.BlockSpec(memory_space=pl.ANY)] * len(groups),
        out_specs=[pl.BlockSpec(memory_space=pltpu.VMEM)] * 2,
        scratch_shapes=[
            pltpu.VMEM((key_rows, dim), jnp.bfloat16),
            pltpu.VMEM((blocks, LANES), jnp.int32),
            pltpu.SMEM((blocks, LANES), jnp.int32),
            pltpu.SMEM((blocks,), jnp.int32),
            pltpu.SemaphoreType.DMA((len(groups),)),
            pltpu.SemaphoreType.DMA,
            pltpu.VMEM((1, dim), jnp.float32),
            pltpu.VMEM((1, dim), jnp.float32),
            pltpu.VMEM((LANES, dim), jnp.float32),
            pltpu.VMEM(square, jnp.float32),
            pltpu.VMEM(square, jnp.float32),
            pltpu.VMEM((LANES, LANES), jnp.float32),
            pltpu.VMEM((LANES, LANES), jnp.float32),
            pltpu.VMEM(square, jnp.bfloat16),
            pltpu.VMEM(square, jnp.bfloat16),
            pltpu.VMEM((CHUNK, dim), jnp.bfloat16),
            pltpu.VMEM((1, block_rows), jnp.float32),
            pltpu.VMEM((block_rows, dim), jnp.float32),
        ],
        compiler_params=pltpu.CompilerParams(vmem_limit_bytes=VMEM_BYTES),
    )(bucket_sizes, states, *groups)
    return logs.reshape(row_count), means


def shards(states, bucket_sizes):
    row_count, dim = states.shape
    block_count = bucket_sizes.shape[0]
    block_rows = row_count // block_count
    in_block = jnp.arange(LIVE_MAX, dtype=jnp.int32)
    own_live = (in_block[None, :] < bucket_sizes[:, None])[:, :, None]
    prefix = states.reshape(block_count, block_rows, dim)[:, :LIVE_MAX]
    sent = jnp.where(own_live, prefix, jnp.bfloat16(DEAD)).reshape(-1, dim)
    groups = gather_rows(sent)
    return local_call(bucket_sizes, states, groups)


def solution(mesh):
    placed = (P("dev", None), P("dev"))
    return jax.shard_map(
        shards, mesh=mesh, in_specs=placed, out_specs=(P("dev"), P("dev", None)), check_vma=False
    )
```
